32 devices in a mesh: groups: 2 (over x), context: 16 (over z, y, core).
Axes of the slice: x: 2, y: 2, z: 4, core: 2. Of those that a mesh axis runs over, the one named last changes fastest.
Arguments:
- encoded: bfloat16 [24576, 1536], P(('groups', 'context')), parts along dimension 0, may hold values from -64 to 64, as said below
- query_weight: bfloat16 [1536, 768], P('context'), may hold values from -0.104613624 to 0.104613624
- key_weight: bfloat16 [1536, 768], P('context'), may hold values from -4 to 4
- value_weight: bfloat16 [1536, 768], P('context'), may hold values from -0.15625 to 0.15625
- out_weight: bfloat16 [1536, 768], P('context'), may hold values from -0.875 to 0.875
- cotangent: bfloat16 [24576, 1536], P(('groups', 'context')), parts along dimension 0, may hold values from -6 to 6
- valid_frames: int32 [2], P('groups'), parts along dimension 0, may hold values from 11536 to 12288
Outputs:
- layer_out: bfloat16 [24576, 1536], P(('groups', 'context')), parts along dimension 0
- encoded_grad: bfloat16 [24576, 1536], P(('groups', 'context')), parts along dimension 0
- query_weight_grad: float32 [3072, 768], P(('groups', 'context')), parts along dimension 0
- key_weight_grad: float32 [3072, 768], P(('groups', 'context')), parts along dimension 0
- value_weight_grad: float32 [3072, 768], P(('groups', 'context')), parts along dimension 0
- out_weight_grad: float32 [3072, 768], P(('groups', 'context')), parts along dimension 0
The draws below stay inside these ranges and needn't reach their ends.
There are 2 independent parts, one for each index of `groups`. The reference program is written for one: setup_inputs(seed, part) draws one part's arguments, and reference() takes and returns one part's arrays. A program takes and returns all parts, laid end to end along the dimension named above; an argument that names none is the same for every part. Nothing has to cross between parts.
Inputs may be any that keep to these rules, and one draw needn't show every extreme that they name: Frames at position valid_frames and later are padding. `encoded`: drawn afresh for each recording.
All inputs are finite; a program needn't handle non-finite values.
Results may differ from the reference program's by a relative error of at most 0.014.
The reference program's roundings to bfloat16 on the way count: a program that leaves them out, or rounds other values in their place, can miss the bound.
Values may be sent and summed in bfloat16 or wider, within the bound.
No kernel may reach another device: no remote copies, remote signals or barrier semaphores. Data moves between devices by JAX's collectives and lax.ppermute only.
A program may use at most 192 MiB of HBM per device.

```python
import math
import jax
import jax.numpy as jnp
from jax import lax

D = 1536
HEADS = 12
HD = 64
BLOCK = 16
LEFT = 16
E = 768
FRAMES_DEV = 768
FRAMES = 12288


def query_base(key):
    normal_part = jax.random.normal(jax.random.fold_in(key, 21), (D, E), jnp.float32)
    return jnp.clip(normal_part, -4.0, 4.0) * D ** (-0.5)


def draw_query_weight(key, part):
    return query_base(key).astype(jnp.bfloat16)


def draw_key_weight(key, part):
    normal_part = jax.random.normal(jax.random.fold_in(key, 22), (D, E), jnp.float32)
    fresh = jnp.clip(normal_part, -4.0, 4.0) * D ** (-0.5)
    return jnp.clip(fresh, -4.0, 4.0).astype(jnp.bfloat16)


def draw_encoded(key, part):
    tile_count = FRAMES // FRAMES_DEV
    normal_part = jnp.clip(jax.random.normal(jax.random.fold_in(key, 1), (FRAMES, D), jnp.float32), -4.0, 4.0)
    row_scale = jnp.exp(jax.random.uniform(jax.random.fold_in(key, 2), (FRAMES, 1), jnp.float32, math.log(0.3), math.log(3.0)))
    col_scale = jnp.exp(jax.random.uniform(jax.random.fold_in(key, 3), (1, D), jnp.float32, math.log(0.3), math.log(3.0)))
    pairing = jax.random.permutation(jax.random.fold_in(key, 4), tile_count)
    row_tile = jnp.arange(FRAMES, dtype=jnp.int32) // FRAMES_DEV
    col_tile = jnp.arange(D, dtype=jnp.int32) // (D // tile_count)
    boosted = jnp.where(pairing[row_tile][:, None] == col_tile[None, :], 3.0, 1.0)
    values = normal_part * col_scale * boosted
    return jnp.clip(values * row_scale, -64.0, 64.0).astype(jnp.bfloat16)


def spiked(drawn, stream_key, source, target, shards_of, factor):
    owner, partner = [(jnp.arange(drawn.shape[axis_at]) // (drawn.shape[axis_at] // shards_of)).reshape([-1 if axis == axis_at else 1 for axis in range(drawn.ndim)]) for axis_at in (source, target)]
    chosen = jax.random.permutation(stream_key, shards_of)[partner]
    strong = (owner == chosen) | (owner == (partner + shards_of // 2) % shards_of)
    return jnp.where(strong, factor * drawn, drawn)


def block_scale(key, dims, cuts, least, high):
    level = 1.0
    for position, blocks in cuts:
        draws = jax.random.uniform(jax.random.fold_in(jax.random.fold_in(key, 6), position), (blocks,), jnp.float32, least / len(cuts), high / len(cuts))
        level = level * jnp.repeat(jnp.exp(draws), dims[position] // blocks).reshape((-1,) + (1,) * (len(dims) - 1 - position))
    return level


def scatter_about(stream_key, dims, width, limit, cuts=(), held_as=jnp.bfloat16):
    values = width * jax.random.normal(stream_key, dims, jnp.float32)
    if cuts:
        values = values * block_scale(stream_key, dims, cuts, -0.22, 0.18)
    return jnp.clip(values, -limit, limit).astype(held_as)


def bell_draw_with(rng, dims, deviation, most, pieces, heavy, kind=jnp.bfloat16):
    result = deviation * jax.random.normal(rng, dims, jnp.float32)
    if pieces:
        result = result * block_scale(rng, dims, pieces, -0.22, 0.18)
    return jnp.clip(spiked(result, jax.random.fold_in(rng, 3), *heavy), -most, most).astype(kind)


def setup_inputs(seed: int = 0, part: int = 0) -> dict:
    streams_of = jax.random.split(jax.random.key(seed), 8)
    part_keys = jax.random.split(jax.random.fold_in(streams_of[7], part), 8)
    return {
        "encoded": draw_encoded(jax.random.fold_in(jax.random.fold_in(streams_of[7], part), 71), part),
        "query_weight": draw_query_weight(jax.random.fold_in(streams_of[7], 71), part),
        "key_weight": draw_key_weight(jax.random.fold_in(streams_of[7], 71), part),
        "value_weight": scatter_about(streams_of[3], (D, E), D ** -0.5, 0.15625, ((0, 16),)),
        "out_weight": scatter_about(streams_of[4], (D, E), (E // 16) ** -0.5, 0.875, ((0, 16),)),
        "cotangent": bell_draw_with(part_keys[5], (FRAMES, D), 1.0, 6.0, ((0, 16),), (0, 1, 16, 2.0)),
        "valid_frames": jax.random.randint(part_keys[6], (1,), FRAMES - FRAMES_DEV + BLOCK, FRAMES + 1).astype(jnp.int32),
    }


epsilon = 1e-05

def normalize(encoded):
    values = encoded.astype(jnp.float32)
    centered = values - lax.optimization_barrier(jnp.mean(values, axis=1, keepdims=True))
    inverse = lax.rsqrt(lax.optimization_barrier(jnp.mean(centered * centered, axis=1, keepdims=True)) + epsilon)
    return (centered * inverse, inverse)

def block_probs(query_rows, key_rows, block_id, valid_count):
    window = (LEFT + 1) * BLOCK
    key_pos = (block_id - LEFT) * BLOCK + jnp.arange(window, dtype=jnp.int32)
    allowed = (key_pos >= 0) & (key_pos < valid_count)
    query_heads = query_rows.astype(jnp.float32).reshape(BLOCK, HEADS, HD)
    key_heads = key_rows.astype(jnp.float32).reshape(window, HEADS, HD)
    scores = jnp.einsum('qhd,khd->hqk', query_heads, key_heads) * HD ** (-0.5)
    scores = jnp.where(allowed[None, None, :], scores, -1e+30)
    row_max = lax.optimization_barrier(jnp.max(scores, axis=2, keepdims=True))
    shifted = jnp.exp(scores - row_max)
    return shifted / lax.optimization_barrier(jnp.sum(shifted, axis=2, keepdims=True))

def reference(encoded, query_weight, key_weight, value_weight, out_weight, cotangent, valid_frames):
    valid_count = valid_frames[0]
    window = (LEFT + 1) * BLOCK
    context_rows = LEFT * BLOCK
    block_count = FRAMES // BLOCK
    row_mask = (jnp.arange(FRAMES, dtype=jnp.int32) < valid_count).astype(jnp.float32)[:, None]
    unit_rows, inverse = normalize(encoded)
    normed = unit_rows.astype(jnp.bfloat16)
    queries = jnp.dot(normed, query_weight, preferred_element_type=jnp.float32).astype(jnp.bfloat16)
    keys = jnp.dot(normed, key_weight, preferred_element_type=jnp.float32).astype(jnp.bfloat16)
    values = jnp.dot(normed, value_weight, preferred_element_type=jnp.float32).astype(jnp.bfloat16)
    padded_keys = jnp.concatenate([jnp.zeros((context_rows, E), jnp.bfloat16), keys], axis=0)
    padded_values = jnp.concatenate([jnp.zeros((context_rows, E), jnp.bfloat16), values], axis=0)

    def forward_block(block_id):
        begin_row = block_id * BLOCK
        query_rows = lax.dynamic_slice_in_dim(queries, begin_row, BLOCK, 0)
        key_rows = lax.dynamic_slice_in_dim(padded_keys, begin_row, window, 0)
        value_rows = lax.dynamic_slice_in_dim(padded_values, begin_row, window, 0)
        attn_probs = block_probs(query_rows, key_rows, block_id, valid_count)
        value_heads = value_rows.astype(jnp.float32).reshape(window, HEADS, HD)
        mixed = jnp.einsum('hqk,khd->qhd', attn_probs.astype(jnp.bfloat16).astype(jnp.float32), value_heads)
        return mixed.reshape(BLOCK, E)
    mixed_all = lax.map(forward_block, jnp.arange(block_count, dtype=jnp.int32)).reshape(FRAMES, E)
    attended = (mixed_all * row_mask).astype(jnp.bfloat16)
    layer_out = (encoded.astype(jnp.float32) + jnp.dot(attended, out_weight.T, preferred_element_type=jnp.float32)).astype(jnp.bfloat16)
    out_weight_grad = jnp.dot(cotangent.T, attended, preferred_element_type=jnp.float32)
    grad_attended = (jnp.dot(cotangent, out_weight, preferred_element_type=jnp.float32) * row_mask).astype(jnp.bfloat16)

    def backward_block(running, block_id):
        key_acc, value_acc = running
        begin_row = block_id * BLOCK
        query_rows = lax.dynamic_slice_in_dim(queries, begin_row, BLOCK, 0)
        key_rows = lax.dynamic_slice_in_dim(padded_keys, begin_row, window, 0)
        value_rows = lax.dynamic_slice_in_dim(padded_values, begin_row, window, 0)
        grad_rows = lax.dynamic_slice_in_dim(grad_attended, begin_row, BLOCK, 0)
        attn_probs = block_probs(query_rows, key_rows, block_id, valid_count)
        grad_heads = grad_rows.astype(jnp.float32).reshape(BLOCK, HEADS, HD)
        value_heads = value_rows.astype(jnp.float32).reshape(window, HEADS, HD)
        key_heads = key_rows.astype(jnp.float32).reshape(window, HEADS, HD)
        query_heads = query_rows.astype(jnp.float32).reshape(BLOCK, HEADS, HD)
        prob_grad = jnp.einsum('qhd,khd->hqk', grad_heads, value_heads)
        row_delta = lax.optimization_barrier(jnp.sum(attn_probs * prob_grad, axis=2, keepdims=True))
        score_grad = (attn_probs * (prob_grad - row_delta) * HD ** (-0.5)).astype(jnp.bfloat16).astype(jnp.float32)
        query_part = jnp.einsum('hqk,khd->qhd', score_grad, key_heads).reshape(BLOCK, E).astype(jnp.bfloat16)
        key_part = jnp.einsum('hqk,qhd->khd', score_grad, query_heads).reshape(window, E)
        value_part = jnp.einsum('hqk,qhd->khd', attn_probs.astype(jnp.bfloat16).astype(jnp.float32), grad_heads).reshape(window, E)
        key_acc = lax.dynamic_update_slice_in_dim(key_acc, lax.dynamic_slice_in_dim(key_acc, begin_row, window, 0) + key_part, begin_row, 0)
        value_acc = lax.dynamic_update_slice_in_dim(value_acc, lax.dynamic_slice_in_dim(value_acc, begin_row, window, 0) + value_part, begin_row, 0)
        return ((key_acc, value_acc), query_part)
    zero_acc = jnp.zeros((FRAMES + context_rows, E), jnp.float32)
    (key_acc, value_acc), query_parts = lax.scan(backward_block, (zero_acc, zero_acc), jnp.arange(block_count, dtype=jnp.int32))
    query_back = query_parts.reshape(FRAMES, E)
    key_back = key_acc[context_rows:].astype(jnp.bfloat16)
    value_back = value_acc[context_rows:].astype(jnp.bfloat16)
    query_weight_grad = jnp.dot(normed.T, query_back, preferred_element_type=jnp.float32)
    key_weight_grad = jnp.dot(normed.T, key_back, preferred_element_type=jnp.float32)
    value_weight_grad = jnp.dot(normed.T, value_back, preferred_element_type=jnp.float32)
    feature_grad = jnp.dot(query_back, query_weight.T, preferred_element_type=jnp.float32)
    feature_grad = feature_grad + jnp.dot(key_back, key_weight.T, preferred_element_type=jnp.float32)
    feature_grad = feature_grad + jnp.dot(value_back, value_weight.T, preferred_element_type=jnp.float32)
    centered_grad = feature_grad - lax.optimization_barrier(jnp.mean(feature_grad, axis=1, keepdims=True)) - unit_rows * lax.optimization_barrier(jnp.mean(feature_grad * unit_rows, axis=1, keepdims=True))
    encoded_grad = (cotangent.astype(jnp.float32) + inverse * centered_grad).astype(jnp.bfloat16)
    return (layer_out, encoded_grad, query_weight_grad, key_weight_grad, value_weight_grad, out_weight_grad)
```

```python
import jax
import jax.numpy as jnp
from jax import lax
from jax.experimental import pallas as pl
from jax.experimental.pallas import tpu as pltpu
from jax.sharding import PartitionSpec as P

HEADS = 12
HD = 64
BLOCK = 16
LEFT = 16
E = 768
SPAN = LEFT * BLOCK
HALF = SPAN // 2
PAIR = 2 * HD
GROUPS = 3

epsilon = 1e-05

F32 = jnp.float32
BF16 = jnp.bfloat16


def passed_along(value, axis, by):
    count = lax.axis_size(axis)
    pairs = [(i, i + by) for i in range(count) if 0 <= i + by < count]
    return lax.ppermute(value, axis, pairs)


def swapped(value, mask):
    count = lax.axis_size("context")
    return lax.ppermute(value, "context", [(i, i ^ mask) for i in range(count)])


def after(value, *others):
    return lax.optimization_barrier((value, *others))[0]


def normalize(encoded):
    values = encoded.astype(F32)
    centered = values - jnp.mean(values, axis=1, keepdims=True)
    inverse = lax.rsqrt(jnp.mean(centered * centered, axis=1, keepdims=True) + epsilon)
    return (centered * inverse, inverse)


def dot_nt(a, b):
    return lax.dot_general(a, b, (((1,), (1,)), ((), ())), preferred_element_type=F32)


def dot_nn(a, b):
    return lax.dot_general(a, b, (((1,), (0,)), ((), ())), preferred_element_type=F32)


def attention_body(
    pos_ref,
    q_ref,
    k_ref,
    v_ref,
    g_ref,
    o_ref,
    dq_ref,
    main_ref,
    tail_ref,
    halo_ref,
    bias_ref,
    kt_ref,
    vt_ref,
    ot_ref,
    dqt_ref,
    p_ref,
    ds_ref,
    acc_ref,
):
    rows = g_ref.shape[0]
    tiles = rows // SPAN
    first = pos_ref[0]
    count = pos_ref[1]

    @pl.when(pl.program_id(0) == 0)
    def _():
        for t in range(tiles):
            for c in range(2):
                key = lax.broadcasted_iota(jnp.int32, (SPAN + HALF, HALF), 0) + c * HALF
                query = lax.broadcasted_iota(jnp.int32, (SPAN + HALF, HALF), 1) + c * HALF
                key_block = key // BLOCK
                query_block = query // BLOCK
                pos = key + (first + (t - 1) * SPAN)
                allowed = (
                    (key_block >= query_block)
                    & (key_block <= query_block + LEFT)
                    & (pos >= 0)
                    & (pos < count)
                )
                bias_ref[t, c] = jnp.where(allowed, 0.0, -1e30)
        p_ref[...] = jnp.zeros_like(p_ref)
        ds_ref[...] = jnp.zeros_like(ds_ref)

    kt_ref[...] = k_ref[...].T
    vt_ref[...] = v_ref[...].T
    lane = lax.broadcasted_iota(jnp.int32, (SPAN, PAIR), 1)
    for t in range(tiles):
        qs = slice(t * SPAN, (t + 1) * SPAN)
        ks = slice(t * SPAN, (t + 2) * SPAN)
        q = q_ref[(t + 1) * SPAN : (t + 2) * SPAN, :] * BF16(HD ** (-0.5))
        g = g_ref[qs, :]
        k = k_ref[ks, :]
        v = v_ref[ks, :]
        q_heads = []
        g_heads = []
        for h in range(2):
            mine = (lane >= HD) if h else (lane < HD)
            q_heads.append(jnp.where(mine, q, jnp.zeros_like(q)))
            g_heads.append(jnp.where(mine, g, jnp.zeros_like(g)))
            s = dot_nt(k, q_heads[h])
            d = dot_nt(v, g_heads[h])
            for c in range(2):
                kr = slice(c * HALF, c * HALF + SPAN + HALF)
                qc = slice(c * HALF, (c + 1) * HALF)
                out = slice(h * SPAN + c * HALF, h * SPAN + (c + 1) * HALF)
                scores = s[kr, qc] + bias_ref[t, c]
                shifted = jnp.exp(scores - jnp.max(scores, axis=0, keepdims=True))
                probs = shifted * (1.0 / jnp.sum(shifted, axis=0, keepdims=True))
                weighted = probs * d[kr, qc]
                delta = jnp.sum(weighted, axis=0, keepdims=True)
                p_ref[kr, out] = probs.astype(BF16)
                ds_ref[kr, out] = (weighted - probs * delta).astype(BF16)
            hs = slice(h * HD, (h + 1) * HD)
            cols = slice(h * SPAN, (h + 1) * SPAN)
            ot_ref[hs, qs] = dot_nn(vt_ref[hs, ks], p_ref[:, cols])
            dqt_ref[hs, qs] = dot_nn(kt_ref[hs, ks], ds_ref[:, cols]) * HD ** (-0.5)
        for i, part in enumerate(
            (
                dot_nn(ds_ref[...], jnp.concatenate(q_heads, axis=0)),
                dot_nn(p_ref[...], jnp.concatenate(g_heads, axis=0)),
            )
        ):
            if t == 0:
                acc_ref[i, ks, :] = part
            else:
                acc_ref[i, t * SPAN : (t + 1) * SPAN, :] += part[:SPAN]
                acc_ref[i, (t + 1) * SPAN : (t + 2) * SPAN, :] = part[SPAN:]
    row = lax.broadcasted_iota(jnp.int32, (rows, PAIR), 0) + first
    o_ref[...] = jnp.where(row < count, ot_ref[...].T, 0.0).astype(BF16)
    dq_ref[...] = dqt_ref[...].T.astype(BF16)
    halo_ref[...] = acc_ref[:, :SPAN, :].astype(BF16)
    main_ref[...] = acc_ref[:, SPAN:rows, :].astype(BF16)
    tail_ref[...] = acc_ref[:, rows:, :]


def attention(pos, projected, grad_attn):
    rows, cols = grad_attn.shape
    ext = rows + SPAN
    steps = cols // PAIR
    sd = jax.ShapeDtypeStruct
    column = lambda part: pl.BlockSpec((ext, PAIR), lambda j: (0, part * steps + j))
    flat = pl.BlockSpec((rows, PAIR), lambda j: (0, j))
    both = lambda r: pl.BlockSpec((2, r, PAIR), lambda j: (0, 0, j))
    return pl.pallas_call(
        attention_body,
        grid=(steps,),
        in_specs=[pl.BlockSpec(memory_space=pltpu.SMEM), column(0), column(1), column(2), flat],
        out_specs=[flat, flat, both(rows - SPAN), both(SPAN), both(SPAN)],
        out_shape=[
            sd((rows, cols), BF16),
            sd((rows, cols), BF16),
            sd((2, rows - SPAN, cols), BF16),
            sd((2, SPAN, cols), F32),
            sd((2, SPAN, cols), BF16),
        ],
        scratch_shapes=[
            pltpu.VMEM((rows // SPAN, 2, SPAN + HALF, HALF), F32),
            pltpu.VMEM((PAIR, ext), BF16),
            pltpu.VMEM((PAIR, ext), BF16),
            pltpu.VMEM((PAIR, rows), F32),
            pltpu.VMEM((PAIR, rows), F32),
            pltpu.VMEM((2 * SPAN, 2 * SPAN), BF16),
            pltpu.VMEM((2 * SPAN, 2 * SPAN), BF16),
            pltpu.VMEM((2, ext, PAIR), F32),
        ],
        compiler_params=pltpu.CompilerParams(
            dimension_semantics=("arbitrary",), vmem_limit_bytes=24 << 20
        ),
        cost_estimate=pl.CostEstimate(
            flops=36 * rows * 2 * SPAN * cols,
            transcendentals=rows * 6 * cols,
            bytes_accessed=18 * rows * cols,
        ),
    )(pos, projected, projected, projected, grad_attn)


def gather_rows(block, gate):
    count = lax.axis_size("context")
    rows, cols = block.shape
    if count % 4 or count & (count - 1):
        whole = lax.all_gather(block, "context", axis=0, tiled=True)
        return whole, whole, whole
    far = count // 4
    me = lax.axis_index("context")
    z, y, c = me // 4, me // 2 % 2, me % 2
    if gate is not None:
        block = after(block, *gate)
    near = jnp.zeros((far, rows, cols), block.dtype)
    parts = [block] + [swapped(block, 4 * k) for k in range(1, far)]
    for k, part in enumerate(parts):
        near = lax.dynamic_update_slice(near, part[None], (z ^ k, 0, 0))
    other = swapped(near, 2)
    mine = jnp.zeros((far, 2, rows, cols), block.dtype)
    mine = lax.dynamic_update_slice(mine, near[:, None], (0, y, 0, 0))
    mine = lax.dynamic_update_slice(mine, other[:, None], (0, 1 - y, 0, 0))
    sibling = swapped(mine, 1)
    whole = jnp.zeros((far, 2, 2, rows, cols), block.dtype)
    whole = lax.dynamic_update_slice(whole, mine[:, :, None], (0, 0, c, 0, 0))
    whole = lax.dynamic_update_slice(whole, sibling[:, :, None], (0, 0, 1 - c, 0, 0))
    return whole.reshape(count * rows, cols), (parts[-1], parts[1]), other


def scatter_sum(partial):
    count = lax.axis_size("context")
    cols = partial.shape[1]
    rows = partial.shape[0] // count
    if count % 4 or count & (count - 1):
        return lax.psum_scatter(partial, "context", scatter_dimension=0, tiled=True).astype(F32)
    far = count // 4
    me = lax.axis_index("context")
    z, y, c = me // 4, me // 2 % 2, me % 2
    pick = lambda value, index, axis: lax.dynamic_index_in_dim(value, index, axis, keepdims=False)
    held = partial.reshape(far, 2, 2, rows, cols)
    got = swapped(pick(held, 1 - c, 2), 1)
    held = (pick(held, c, 2).astype(F32) + got.astype(F32)).astype(BF16)
    got = swapped(pick(held, 1 - y, 1), 2)
    held = (pick(held, y, 1).astype(F32) + got.astype(F32)).astype(BF16)
    total = pick(held, z, 0).astype(F32)
    for k in range(1, far):
        total = total + swapped(pick(held, z ^ k, 0), 4 * k).astype(F32)
    return total


def shards(encoded, query_weight, key_weight, value_weight, out_weight, cotangent, valid_frames):
    valid_count = valid_frames[0]
    frames_dev = encoded.shape[0]
    cols = E // GROUPS
    first_row = lax.axis_index("context") * frames_dev
    pos = jnp.stack([first_row.astype(jnp.int32), valid_count])
    row_mask = (first_row + jnp.arange(frames_dev, dtype=jnp.int32) < valid_count).astype(F32)[
        :, None
    ]
    left = passed_along(encoded[frames_dev - SPAN :], "context", 1)
    weights = []
    gate = None
    for i in range(GROUPS):
        part = slice(i * cols, (i + 1) * cols)
        block = jnp.concatenate(
            [query_weight[:, part], key_weight[:, part], value_weight[:, part], out_weight[:, part]],
            axis=1,
        )
        whole, gate, _ = gather_rows(block, gate)
        weights.append(whole)
    unit_rows, inverse = normalize(encoded)
    normed = unit_rows.astype(BF16)
    left_normed = normalize(left)[0].astype(BF16)
    normed_ext = jnp.concatenate([left_normed, normed], axis=0)
    attended = []
    backs = []
    in_grads = []
    for i in range(GROUPS):
        whole = weights[i]
        projected = jnp.dot(
            normed_ext, whole[:, : 3 * cols], preferred_element_type=F32
        ).astype(BF16)
        grad_attn = jnp.dot(cotangent, whole[:, 3 * cols :], preferred_element_type=F32)
        grad_attn = (grad_attn * row_mask).astype(BF16)
        mixed, query_back, main, tail, halo = attention(pos, projected, grad_attn)
        returned = passed_along(halo, "context", -1)
        tail = (tail + returned.astype(F32)).astype(BF16)
        back = jnp.concatenate(
            [
                query_back,
                jnp.concatenate([main[0], tail[0]], axis=0),
                jnp.concatenate([main[1], tail[1]], axis=0),
            ],
            axis=1,
        )
        partial = jnp.concatenate(
            [
                jnp.einsum("fc,fe->ce", normed, back, preferred_element_type=F32),
                jnp.einsum("fc,fe->ce", cotangent, mixed, preferred_element_type=F32),
            ],
            axis=1,
        ).astype(BF16)
        in_grads.append(scatter_sum(partial))
        attended.append(mixed)
        backs.append(back)
    projected_out = sum(
        jnp.einsum("fe,de->fd", attended[i], weights[i][:, 3 * cols :], preferred_element_type=F32)
        for i in range(GROUPS)
    )
    layer_out = (encoded.astype(F32) + projected_out).astype(BF16)
    feature_grad = sum(
        jnp.einsum("fe,de->fd", backs[i], weights[i][:, : 3 * cols], preferred_element_type=F32)
        for i in range(GROUPS)
    )
    centered_grad = (
        feature_grad
        - jnp.mean(feature_grad, axis=1, keepdims=True)
        - unit_rows * jnp.mean(feature_grad * unit_rows, axis=1, keepdims=True)
    )
    encoded_grad = (cotangent.astype(F32) + inverse * centered_grad).astype(BF16)
    grads = [
        jnp.concatenate([g[:, k * cols : (k + 1) * cols] for g in in_grads], axis=1)
        for k in range(4)
    ]
    return (layer_out, encoded_grad, *grads)


def solution(mesh):
    placed = (
        P(("groups", "context"), None),
        P("context", None),
        P("context", None),
        P("context", None),
        P("context", None),
        P(("groups", "context"), None),
        P("groups"),
    )
    return jax.shard_map(
        shards,
        mesh=mesh,
        in_specs=placed,
        out_specs=(P(("groups", "context"), None),) * 6,
        check_vma=False,
    )
```

```python
import jax
import jax.numpy as jnp
from jax import lax
from jax.experimental import pallas as pl
from jax.experimental.pallas import tpu as pltpu
from jax.sharding import PartitionSpec as P

HEADS = 12
HD = 64
BLOCK = 16
LEFT = 16
E = 768
SPAN = LEFT * BLOCK
HALF = SPAN // 2
PAIR = 2 * HD
GROUPS = 3

epsilon = 1e-05

F32 = jnp.float32
BF16 = jnp.bfloat16

SCALE = 0.3


def hint(us):
    return pl.CostEstimate(flops=int(SCALE * us * 1.15e9), transcendentals=0, bytes_accessed=1 << 10)


def passed_along(value, axis, by):
    count = lax.axis_size(axis)
    pairs = [(i, i + by) for i in range(count) if 0 <= i + by < count]
    return lax.ppermute(value, axis, pairs)


def swapped(value, mask):
    count = lax.axis_size("context")
    return lax.ppermute(value, "context", [(i, i ^ mask) for i in range(count)])


def after(value, *others):
    return lax.optimization_barrier((value, *others))[0]


def normalize_values(values):
    centered = values - jnp.mean(values, axis=1, keepdims=True)
    inverse = lax.rsqrt(jnp.mean(centered * centered, axis=1, keepdims=True) + epsilon)
    return (centered * inverse, inverse)


def dot_nt(a, b):
    return lax.dot_general(a, b, (((1,), (1,)), ((), ())), preferred_element_type=F32)


def dot_nn(a, b):
    return lax.dot_general(a, b, (((1,), (0,)), ((), ())), preferred_element_type=F32)


def attention_body(
    pos_ref,
    q_ref,
    k_ref,
    v_ref,
    g_ref,
    o_ref,
    dq_ref,
    main_ref,
    tail_ref,
    halo_ref,
    bias_ref,
    kt_ref,
    vt_ref,
    ot_ref,
    dqt_ref,
    p_ref,
    ds_ref,
    acc_ref,
):
    rows = g_ref.shape[0]
    tiles = rows // SPAN
    first = pos_ref[0]
    count = pos_ref[1]

    @pl.when(pl.program_id(0) == 0)
    def _():
        for t in range(tiles):
            for c in range(2):
                key = lax.broadcasted_iota(jnp.int32, (SPAN + HALF, HALF), 0) + c * HALF
                query = lax.broadcasted_iota(jnp.int32, (SPAN + HALF, HALF), 1) + c * HALF
                key_block = key // BLOCK
                query_block = query // BLOCK
                pos = key + (first + (t - 1) * SPAN)
                allowed = (
                    (key_block >= query_block)
                    & (key_block <= query_block + LEFT)
                    & (pos >= 0)
                    & (pos < count)
                )
                bias_ref[t, c] = jnp.where(allowed, 0.0, -1e30)
        p_ref[...] = jnp.zeros_like(p_ref)
        ds_ref[...] = jnp.zeros_like(ds_ref)

    kt_ref[...] = k_ref[...].T
    vt_ref[...] = v_ref[...].T
    lane = lax.broadcasted_iota(jnp.int32, (SPAN, PAIR), 1)
    for t in range(tiles):
        qs = slice(t * SPAN, (t + 1) * SPAN)
        ks = slice(t * SPAN, (t + 2) * SPAN)
        q = q_ref[(t + 1) * SPAN : (t + 2) * SPAN, :] * BF16(HD ** (-0.5))
        g = g_ref[qs, :]
        k = k_ref[ks, :]
        v = v_ref[ks, :]
        q_heads = []
        g_heads = []
        for h in range(2):
            mine = (lane >= HD) if h else (lane < HD)
            q_heads.append(jnp.where(mine, q, jnp.zeros_like(q)))
            g_heads.append(jnp.where(mine, g, jnp.zeros_like(g)))
            s = dot_nt(k, q_heads[h])
            d = dot_nt(v, g_heads[h])
            for c in range(2):
                kr = slice(c * HALF, c * HALF + SPAN + HALF)
                qc = slice(c * HALF, (c + 1) * HALF)
                out = slice(h * SPAN + c * HALF, h * SPAN + (c + 1) * HALF)
                scores = s[kr, qc] + bias_ref[t, c]
                shifted = jnp.exp(scores - jnp.max(scores, axis=0, keepdims=True))
                probs = shifted * (1.0 / jnp.sum(shifted, axis=0, keepdims=True))
                weighted = probs * d[kr, qc]
                delta = jnp.sum(weighted, axis=0, keepdims=True)
                p_ref[kr, out] = probs.astype(BF16)
                ds_ref[kr, out] = (weighted - probs * delta).astype(BF16)
            hs = slice(h * HD, (h + 1) * HD)
            cols = slice(h * SPAN, (h + 1) * SPAN)
            ot_ref[hs, qs] = dot_nn(vt_ref[hs, ks], p_ref[:, cols])
            dqt_ref[hs, qs] = dot_nn(kt_ref[hs, ks], ds_ref[:, cols]) * HD ** (-0.5)
        for i, part in enumerate(
            (
                dot_nn(ds_ref[...], jnp.concatenate(q_heads, axis=0)),
                dot_nn(p_ref[...], jnp.concatenate(g_heads, axis=0)),
            )
        ):
            if t == 0:
                acc_ref[i, ks, :] = part
            else:
                acc_ref[i, t * SPAN : (t + 1) * SPAN, :] += part[:SPAN]
                acc_ref[i, (t + 1) * SPAN : (t + 2) * SPAN, :] = part[SPAN:]
    row = lax.broadcasted_iota(jnp.int32, (rows, PAIR), 0) + first
    o_ref[...] = jnp.where(row < count, ot_ref[...].T, 0.0).astype(BF16)
    dq_ref[...] = dqt_ref[...].T.astype(BF16)
    halo_ref[...] = acc_ref[:, :SPAN, :].astype(BF16)
    main_ref[...] = acc_ref[:, SPAN:rows, :].astype(BF16)
    tail_ref[...] = acc_ref[:, rows:, :]


def attention(pos, projected, grad_attn):
    rows, cols = grad_attn.shape
    ext = rows + SPAN
    steps = cols // PAIR
    sd = jax.ShapeDtypeStruct
    column = lambda part: pl.BlockSpec((ext, PAIR), lambda j: (0, part * steps + j))
    flat = pl.BlockSpec((rows, PAIR), lambda j: (0, j))
    both = lambda r: pl.BlockSpec((2, r, PAIR), lambda j: (0, 0, j))
    return pl.pallas_call(
        attention_body,
        grid=(steps,),
        in_specs=[pl.BlockSpec(memory_space=pltpu.SMEM), column(0), column(1), column(2), flat],
        out_specs=[flat, flat, both(rows - SPAN), both(SPAN), both(SPAN)],
        out_shape=[
            sd((rows, cols), BF16),
            sd((rows, cols), BF16),
            sd((2, rows - SPAN, cols), BF16),
            sd((2, SPAN, cols), F32),
            sd((2, SPAN, cols), BF16),
        ],
        scratch_shapes=[
            pltpu.VMEM((rows // SPAN, 2, SPAN + HALF, HALF), F32),
            pltpu.VMEM((PAIR, ext), BF16),
            pltpu.VMEM((PAIR, ext), BF16),
            pltpu.VMEM((PAIR, rows), F32),
            pltpu.VMEM((PAIR, rows), F32),
            pltpu.VMEM((2 * SPAN, 2 * SPAN), BF16),
            pltpu.VMEM((2 * SPAN, 2 * SPAN), BF16),
            pltpu.VMEM((2, ext, PAIR), F32),
        ],
        compiler_params=pltpu.CompilerParams(
            dimension_semantics=("arbitrary",), vmem_limit_bytes=24 << 20
        ),
        cost_estimate=hint(9.4),
    )(pos, projected, projected, projected, grad_attn)


def order_of(count):
    if count < 4 or count & (count - 1):
        raise ValueError("context size")
    far = count // 4
    return [4 * k + 2 * y + c for c in range(2) for y in range(2) for k in range(far)]


def prepare(me, left, encoded, cotangent, order):
    frames, width = encoded.shape
    count = len(order)
    rows = width // count
    steps = frames // SPAN + 1

    def body(me_ref, left_ref, own_ref, cot_ref, x_ref, c_ref, xt_ref, ct_ref, turned_ref):
        step = pl.program_id(0)
        here = me_ref[0]

        def place(out_ref, flat_ref, value):
            turned_ref[...] = value.T
            for j, offset in enumerate(order):
                source = pl.multiple_of((here ^ offset) * rows, rows)
                out_ref[j * rows : (j + 1) * rows, :] = turned_ref[pl.ds(source, rows), :]
            flat_ref[...] = out_ref[...].T

        values = jnp.where(step == 0, left_ref[...].astype(F32), own_ref[...].astype(F32))
        place(xt_ref, x_ref, normalize_values(values)[0].astype(BF16))

        @pl.when(step > 0)
        def _():
            place(ct_ref, c_ref, cot_ref[...])

    before = lambda i: jnp.maximum(i - 1, 0)
    sd = jax.ShapeDtypeStruct
    return pl.pallas_call(
        body,
        grid=(steps,),
        in_specs=[
            pl.BlockSpec(memory_space=pltpu.SMEM),
            pl.BlockSpec((SPAN, width), lambda i: (0, 0)),
            pl.BlockSpec((SPAN, width), lambda i: (before(i), 0)),
            pl.BlockSpec((SPAN, width), lambda i: (before(i), 0)),
        ],
        out_specs=[
            pl.BlockSpec((SPAN, width), lambda i: (i, 0)),
            pl.BlockSpec((SPAN, width), lambda i: (before(i), 0)),
            pl.BlockSpec((width, SPAN), lambda i: (0, i)),
            pl.BlockSpec((width, SPAN), lambda i: (0, before(i))),
        ],
        out_shape=[
            sd((frames + SPAN, width), BF16),
            sd((frames, width), BF16),
            sd((width, frames + SPAN), BF16),
            sd((width, frames), BF16),
        ],
        scratch_shapes=[pltpu.VMEM((width, SPAN), BF16)],
        compiler_params=pltpu.CompilerParams(
            dimension_semantics=("arbitrary",), vmem_limit_bytes=24 << 20
        ),
        cost_estimate=hint(6.4),
    )(me, left, encoded, cotangent)


def gradients_body(
    xt_ref, ct_ref, query_ref, main_ref, tail_ref, returned_ref, mixed_ref, keep_ref, send_ref, back_ref
):
    step = pl.program_id(0)
    half = pl.num_programs(0) // 2
    rows, cols = query_ref.shape

    @pl.when(step == 0)
    def _():
        back_ref[:, :cols] = query_ref[...]
        for i in range(2):
            part = slice((i + 1) * cols, (i + 2) * cols)
            back_ref[: rows - SPAN, part] = main_ref[i]
            back_ref[rows - SPAN :, part] = (tail_ref[i] + returned_ref[i].astype(F32)).astype(BF16)

    inner = dot_nn(xt_ref[:, SPAN:], back_ref[...]).astype(BF16)
    outer = dot_nn(ct_ref[...], mixed_ref[...]).astype(BF16)

    @pl.when(step < half)
    def _():
        keep_ref[:, : 3 * cols] = inner
        keep_ref[:, 3 * cols :] = outer

    @pl.when(step >= half)
    def _():
        send_ref[:, : 3 * cols] = inner
        send_ref[:, 3 * cols :] = outer


def gradients(xt, ct, query_back, main, tail, returned, mixed):
    width, ext = xt.shape
    rows, cols = mixed.shape
    tile = 256
    steps = width // tile
    whole = lambda a: pl.BlockSpec(a.shape, lambda i: (0,) * a.ndim)
    sd = jax.ShapeDtypeStruct
    return pl.pallas_call(
        gradients_body,
        grid=(steps,),
        in_specs=[
            pl.BlockSpec((tile, ext), lambda i: (i, 0)),
            pl.BlockSpec((tile, rows), lambda i: (i, 0)),
            *(whole(a) for a in (query_back, main, tail, returned, mixed)),
        ],
        out_specs=[
            pl.BlockSpec((tile, 4 * cols), lambda i: (jnp.minimum(i, steps // 2 - 1), 0)),
            pl.BlockSpec((tile, 4 * cols), lambda i: (jnp.maximum(i - steps // 2, 0), 0)),
            pl.BlockSpec((rows, 3 * cols), lambda i: (0, 0)),
        ],
        out_shape=[
            sd((width // 2, 4 * cols), BF16),
            sd((width // 2, 4 * cols), BF16),
            sd((rows, 3 * cols), BF16),
        ],
        compiler_params=pltpu.CompilerParams(
            dimension_semantics=("arbitrary",), vmem_limit_bytes=24 << 20
        ),
        cost_estimate=hint(4.0),
    )(xt, ct, query_back, main, tail, returned, mixed)


def fetch(me_ref, weight_refs, held_ref, sem, first, cols, count):
    here = me_ref[0]
    rows = held_ref.shape[1] // count
    copies = []
    for d in range(count):
        apart = here ^ d
        j = apart % 2 * (count // 2) + apart // 2 % 2 * (count // 4) + apart // 4
        source = pl.multiple_of(j * rows, rows)
        copies.append(
            [
                pltpu.make_async_copy(
                    weight_ref.at[pl.ds(source, rows), first : first + cols],
                    held_ref.at[g, d * rows : (d + 1) * rows, :],
                    sem.at[g, d],
                )
                for g, weight_ref in enumerate(weight_refs)
            ]
        )
    for some in copies:
        for copy in some:
            copy.start()
    return copies


def finish_out(me, encoded, attended, weights, count):
    frames, width = encoded.shape
    cols = attended[0].shape[1]
    groups = len(weights)
    rows = width // count
    tile = 256

    def body(me_ref, enc_ref, *refs):
        mixed_refs = refs[:groups]
        weight_refs = refs[groups : 2 * groups]
        out_ref, held_ref, sem = refs[2 * groups :]
        copies = fetch(me_ref, weight_refs, held_ref, sem, 3 * cols, cols, count)
        waited = 0
        for t in range(width // tile):
            part = slice(t * tile, (t + 1) * tile)
            while waited * rows < (t + 1) * tile:
                for copy in copies[waited]:
                    copy.wait()
                waited += 1
            projected = enc_ref[:, part].astype(F32)
            for g in range(groups):
                projected = projected + dot_nt(mixed_refs[g][...], held_ref[g, part, :])
            out_ref[:, part] = projected.astype(BF16)

    vmem = pl.BlockSpec(memory_space=pltpu.VMEM)
    return pl.pallas_call(
        body,
        in_specs=[
            pl.BlockSpec(memory_space=pltpu.SMEM),
            *(vmem for _ in range(1 + groups)),
            *(pl.BlockSpec(memory_space=pl.ANY) for _ in range(groups)),
        ],
        out_specs=vmem,
        out_shape=jax.ShapeDtypeStruct((frames, width), BF16),
        scratch_shapes=[
            pltpu.VMEM((groups, width, cols), BF16),
            pltpu.SemaphoreType.DMA((groups, count)),
        ],
        compiler_params=pltpu.CompilerParams(vmem_limit_bytes=24 << 20),
        cost_estimate=hint(7.0),
    )(me, encoded, *attended, *weights)


def finish_grad(me, encoded, cotangent, backs, weights, count):
    frames, width = encoded.shape
    cols = backs[0].shape[1] // 3
    groups = len(weights)
    rows = width // count
    tile = 256

    def body(me_ref, enc_ref, cot_ref, *refs):
        back_refs = refs[:groups]
        weight_refs = refs[groups : 2 * groups]
        grad_ref, held_ref, feature_ref, sem = refs[2 * groups :]
        copies = fetch(me_ref, weight_refs, held_ref, sem, 0, 3 * cols, count)
        values = enc_ref[...].astype(F32)
        mean = jnp.mean(values, axis=1, keepdims=True)
        centered = values - mean
        inverse = lax.rsqrt(jnp.mean(centered * centered, axis=1, keepdims=True) + epsilon)
        first = jnp.zeros((frames, 1), F32)
        second = jnp.zeros((frames, 1), F32)
        waited = 0
        for t in range(width // tile):
            part = slice(t * tile, (t + 1) * tile)
            while waited * rows < (t + 1) * tile:
                for copy in copies[waited]:
                    copy.wait()
                waited += 1
            feature = dot_nt(back_refs[0][...], held_ref[0, part, :])
            for g in range(1, groups):
                feature = feature + dot_nt(back_refs[g][...], held_ref[g, part, :])
            feature_ref[:, part] = feature
            unit_rows = (enc_ref[:, part].astype(F32) - mean) * inverse
            first = first + jnp.sum(feature, axis=1, keepdims=True)
            second = second + jnp.sum(feature * unit_rows, axis=1, keepdims=True)
        first = first * (1.0 / width)
        second = second * (1.0 / width)
        for t in range(width // tile):
            part = slice(t * tile, (t + 1) * tile)
            unit_rows = (enc_ref[:, part].astype(F32) - mean) * inverse
            centered_grad = feature_ref[:, part] - first - unit_rows * second
            grad_ref[:, part] = (cot_ref[:, part].astype(F32) + inverse * centered_grad).astype(BF16)

    vmem = pl.BlockSpec(memory_space=pltpu.VMEM)
    return pl.pallas_call(
        body,
        in_specs=[
            pl.BlockSpec(memory_space=pltpu.SMEM),
            *(vmem for _ in range(2 + groups)),
            *(pl.BlockSpec(memory_space=pl.ANY) for _ in range(groups)),
        ],
        out_specs=vmem,
        out_shape=jax.ShapeDtypeStruct((frames, width), BF16),
        scratch_shapes=[
            pltpu.VMEM((groups, width, 3 * cols), BF16),
            pltpu.VMEM((frames, width), F32),
            pltpu.SemaphoreType.DMA((groups, count)),
        ],
        compiler_params=pltpu.CompilerParams(vmem_limit_bytes=36 << 20),
        cost_estimate=hint(14.0),
    )(me, encoded, cotangent, *backs, *weights)


def collect(sums, cols):
    groups = len(sums)
    peers = len(sums[0][1])
    rows = sums[0][0].shape[0]

    def body(*refs):
        outs = refs[-4:]
        for g in range(groups):
            own, *parts = refs[g * (peers + 1) : (g + 1) * (peers + 1)]
            total = own[...]
            for part in parts:
                total = total + part[...].astype(F32)
            for k in range(4):
                outs[k][:, g * cols : (g + 1) * cols] = total[:, k * cols : (k + 1) * cols]

    flat = [a for own, parts in sums for a in (own, *parts)]
    vmem = pl.BlockSpec(memory_space=pltpu.VMEM)
    return pl.pallas_call(
        body,
        in_specs=[vmem] * len(flat),
        out_specs=[vmem] * 4,
        out_shape=[jax.ShapeDtypeStruct((rows, groups * cols), F32)] * 4,
        compiler_params=pltpu.CompilerParams(vmem_limit_bytes=16 << 20),
        cost_estimate=hint(1.2),
    )(*flat)


def shards(encoded, query_weight, key_weight, value_weight, out_weight, cotangent, valid_frames):
    valid_count = valid_frames[0]
    frames_dev = encoded.shape[0]
    cols = E // GROUPS
    count = lax.axis_size("context")
    far = count // 4
    order = order_of(count)
    index = lax.axis_index("context").astype(jnp.int32)
    first_row = index * frames_dev
    me = index[None]
    pos = jnp.stack([first_row, valid_count])
    row_mask = (first_row + jnp.arange(frames_dev, dtype=jnp.int32) < valid_count).astype(F32)[
        :, None
    ]
    left = passed_along(encoded[frames_dev - SPAN :], "context", 1)
    sources = (query_weight, key_weight, value_weight, out_weight)

    def block_of(i, sources):
        part = slice(i * cols, (i + 1) * cols)
        return jnp.concatenate([w[:, part] for w in sources], axis=1)

    raw, near, other, weights = ([None] * GROUPS for _ in range(4))

    def gather_far(i, *gate):
        block = block_of(i, lax.optimization_barrier((*sources, *gate))[:4] if gate else sources)
        raw[i] = (block, *(swapped(block, 4 * k) for k in range(1, far)))

    def join_far(i, *gate):
        parts = after(raw[i], *gate) if gate else raw[i]
        near[i] = jnp.concatenate(parts, axis=0)

    def gather_next(i, *gate):
        if gate:
            near[i] = after(near[i], *gate)
        other[i] = swapped(near[i], 2)

    def gather_chip(i, *gate):
        if gate:
            other[i] = after(other[i], *gate)
        mine = jnp.concatenate([near[i], other[i]], axis=0)
        weights[i] = jnp.concatenate([mine, swapped(mine, 1)], axis=0)

    x, c, xt, ct = prepare(me, left, encoded, cotangent, order)
    gather_far(0)
    join_far(0, left)
    gather_next(0)
    gather_far(1, near[0])
    join_far(1)
    gather_chip(0, near[1])
    gather_next(1, other[0])
    gather_far(2, near[1], other[0])

    def project(i, *gate):
        whole = after(weights[i], *gate) if gate else weights[i]
        projected = jnp.dot(x, whole[:, : 3 * cols], preferred_element_type=F32).astype(BF16)
        grad_attn = jnp.dot(c, whole[:, 3 * cols :], preferred_element_type=F32)
        return projected, (grad_attn * row_mask).astype(BF16)

    attended, backs, keeps, sends, sums = [], [], [], [], []

    def sum_chip(i):
        total = keeps[i].astype(F32) + swapped(sends[i], 1).astype(F32)
        half = total.shape[0] // 2
        return total[:half], total[half:].astype(BF16)

    def split_far(held, got):
        total = held + got.astype(F32)
        rows = total.shape[0] // far
        return total[:rows], [total[k * rows : (k + 1) * rows].astype(BF16) for k in range(1, far)]

    held = got = own = parts = None
    for i in range(GROUPS):
        projected, grad_attn = project(i, *((keeps[i - 1],) if i else ()))
        if i:
            held, send = sum_chip(i - 1)
            held, send, projected = lax.optimization_barrier((held, send, projected))
            got = swapped(send, 2)
        if i > 1:
            parts, projected = lax.optimization_barrier((parts, projected))
            sums.append((own, parts))
        mixed, query_back, main, tail, halo = attention(pos, projected, grad_attn)
        attended.append(mixed)
        returned = passed_along(halo, "context", -1)
        if i + 1 < GROUPS:
            if i + 2 < GROUPS:
                join_far(i + 2, mixed)
            gather_chip(i + 1, mixed, *(near[i + 2 : i + 3]))
        if i + 2 < GROUPS:
            gather_next(i + 2, mixed, other[i + 1])
        if i:
            held, got, mixed = lax.optimization_barrier((held, got, mixed))
            own, away = split_far(held, got)
            parts = [swapped(part, 4 * k) for k, part in enumerate(away, 1)]
        keep, send, back = gradients(xt, ct, query_back, main, tail, returned, mixed)
        keeps.append(keep)
        sends.append(send)
        backs.append(back)
    held, send = sum_chip(GROUPS - 1)
    held, send, ready = lax.optimization_barrier((held, send, me))
    got = swapped(send, 2)
    layer_out = finish_out(ready, encoded, attended, weights, count)
    got, parts, layer_out = lax.optimization_barrier((got, parts, layer_out))
    sums.append((own, parts))
    own, away = split_far(held, got)
    *away, ready = lax.optimization_barrier((*away, me))
    parts = [swapped(part, 4 * k) for k, part in enumerate(away, 1)]
    encoded_grad = finish_grad(ready, encoded, cotangent, backs, weights, count)
    parts, encoded_grad = lax.optimization_barrier((parts, encoded_grad))
    sums.append((own, parts))
    return (layer_out, encoded_grad, *collect(sums, cols))


def solution(mesh):
    placed = (
        P(("groups", "context"), None),
        P("context", None),
        P("context", None),
        P("context", None),
        P("context", None),
        P(("groups", "context"), None),
        P("groups"),
    )
    return jax.shard_map(
        shards,
        mesh=mesh,
        in_specs=placed,
        out_specs=(P(("groups", "context"), None),) * 6,
        check_vma=False,
    )
```

```python
import jax
import jax.numpy as jnp
from jax import lax
from jax.experimental import pallas as pl
from jax.experimental.pallas import tpu as pltpu
from jax.sharding import PartitionSpec as P

HEADS = 12
HD = 64
BLOCK = 16
LEFT = 16
E = 768
SPAN = LEFT * BLOCK
HALF = SPAN // 2
PAIR = 2 * HD
SIZES = (4, 4, 4)
GROUPS = len(SIZES)
WIDTHS = tuple(HD * size for size in SIZES)
STARTS = tuple(sum(WIDTHS[:i]) for i in range(GROUPS))

epsilon = 1e-05

F32 = jnp.float32
BF16 = jnp.bfloat16

SCALE = 0.3


def hint(us):
    return pl.CostEstimate(flops=int(SCALE * us * 1.15e9), transcendentals=0, bytes_accessed=1 << 10)


def passed_along(value, axis, by):
    count = lax.axis_size(axis)
    pairs = [(i, i + by) for i in range(count) if 0 <= i + by < count]
    return lax.ppermute(value, axis, pairs)


def swapped(value, mask):
    count = lax.axis_size("context")
    return lax.ppermute(value, "context", [(i, i ^ mask) for i in range(count)])


def after(value, *others):
    return lax.optimization_barrier((value, *others))[0]


def normalize_values(values):
    centered = values - jnp.mean(values, axis=1, keepdims=True)
    inverse = lax.rsqrt(jnp.mean(centered * centered, axis=1, keepdims=True) + epsilon)
    return (centered * inverse, inverse)


def dot_nt(a, b):
    return lax.dot_general(a, b, (((1,), (1,)), ((), ())), preferred_element_type=F32)


def dot_nn(a, b):
    return lax.dot_general(a, b, (((1,), (0,)), ((), ())), preferred_element_type=F32)


def attention_body(
    pos_ref,
    q_ref,
    k_ref,
    v_ref,
    g_ref,
    o_ref,
    dq_ref,
    main_ref,
    tail_ref,
    halo_ref,
    bias_ref,
    kt_ref,
    vt_ref,
    ot_ref,
    dqt_ref,
    p_ref,
    ds_ref,
    acc_ref,
):
    rows = g_ref.shape[0]
    tiles = rows // SPAN
    first = pos_ref[0]
    count = pos_ref[1]

    @pl.when(pl.program_id(0) == 0)
    def _():
        for t in range(tiles):
            for c in range(2):
                key = lax.broadcasted_iota(jnp.int32, (SPAN + HALF, HALF), 0) + c * HALF
                query = lax.broadcasted_iota(jnp.int32, (SPAN + HALF, HALF), 1) + c * HALF
                key_block = key // BLOCK
                query_block = query // BLOCK
                pos = key + (first + (t - 1) * SPAN)
                allowed = (
                    (key_block >= query_block)
                    & (key_block <= query_block + LEFT)
                    & (pos >= 0)
                    & (pos < count)
                )
                bias_ref[t, c] = jnp.where(allowed, 0.0, -1e30)
        p_ref[...] = jnp.zeros_like(p_ref)
        ds_ref[...] = jnp.zeros_like(ds_ref)

    kt_ref[...] = k_ref[...].T
    vt_ref[...] = v_ref[...].T
    lane = lax.broadcasted_iota(jnp.int32, (SPAN, PAIR), 1)
    acc_ref[...] = jnp.zeros_like(acc_ref)

    def one_tile(t, carry):
        start = pl.multiple_of(t * SPAN, SPAN)
        qs = pl.ds(start, SPAN)
        ks = pl.ds(start, 2 * SPAN)
        q = q_ref[pl.ds(start + SPAN, SPAN), :] * BF16(HD ** (-0.5))
        g = g_ref[qs, :]
        k = k_ref[ks, :]
        v = v_ref[ks, :]
        q_heads = []
        g_heads = []
        for h in range(2):
            mine = (lane >= HD) if h else (lane < HD)
            q_heads.append(jnp.where(mine, q, jnp.zeros_like(q)))
            g_heads.append(jnp.where(mine, g, jnp.zeros_like(g)))
            s = dot_nt(k, q_heads[h])
            d = dot_nt(v, g_heads[h])
            for c in range(2):
                kr = slice(c * HALF, c * HALF + SPAN + HALF)
                qc = slice(c * HALF, (c + 1) * HALF)
                out = slice(h * SPAN + c * HALF, h * SPAN + (c + 1) * HALF)
                scores = s[kr, qc] + bias_ref[t, c]
                shifted = jnp.exp(scores - jnp.max(scores, axis=0, keepdims=True))
                probs = shifted * (1.0 / jnp.sum(shifted, axis=0, keepdims=True))
                weighted = probs * d[kr, qc]
                delta = jnp.sum(weighted, axis=0, keepdims=True)
                p_ref[kr, out] = probs.astype(BF16)
                ds_ref[kr, out] = (weighted - probs * delta).astype(BF16)
            hs = slice(h * HD, (h + 1) * HD)
            cols = slice(h * SPAN, (h + 1) * SPAN)
            ot_ref[hs, qs] = dot_nn(vt_ref[hs, ks], p_ref[:, cols])
            dqt_ref[hs, qs] = dot_nn(kt_ref[hs, ks], ds_ref[:, cols]) * HD ** (-0.5)
        acc_ref[0, ks, :] += dot_nn(ds_ref[...], jnp.concatenate(q_heads, axis=0))
        acc_ref[1, ks, :] += dot_nn(p_ref[...], jnp.concatenate(g_heads, axis=0))
        return carry

    lax.fori_loop(0, tiles, one_tile, 0, unroll=True)
    row = lax.broadcasted_iota(jnp.int32, (rows, PAIR), 0) + first
    o_ref[...] = jnp.where(row < count, ot_ref[...].T, 0.0).astype(BF16)
    dq_ref[...] = dqt_ref[...].T.astype(BF16)
    halo_ref[...] = acc_ref[:, :SPAN, :].astype(BF16)
    main_ref[...] = acc_ref[:, SPAN:rows, :].astype(BF16)
    tail_ref[...] = acc_ref[:, rows:, :]


def attention(pos, projected, grad_attn):
    rows, cols = grad_attn.shape
    ext = rows + SPAN
    steps = cols // PAIR
    sd = jax.ShapeDtypeStruct
    column = lambda part: pl.BlockSpec((ext, PAIR), lambda j: (0, part * steps + j))
    flat = pl.BlockSpec((rows, PAIR), lambda j: (0, j))
    both = lambda r: pl.BlockSpec((2, r, PAIR), lambda j: (0, 0, j))
    return pl.pallas_call(
        attention_body,
        grid=(steps,),
        in_specs=[pl.BlockSpec(memory_space=pltpu.SMEM), column(0), column(1), column(2), flat],
        out_specs=[flat, flat, both(rows - SPAN), both(SPAN), both(SPAN)],
        out_shape=[
            sd((rows, cols), BF16),
            sd((rows, cols), BF16),
            sd((2, rows - SPAN, cols), BF16),
            sd((2, SPAN, cols), F32),
            sd((2, SPAN, cols), BF16),
        ],
        scratch_shapes=[
            pltpu.VMEM((rows // SPAN, 2, SPAN + HALF, HALF), F32),
            pltpu.VMEM((PAIR, ext), BF16),
            pltpu.VMEM((PAIR, ext), BF16),
            pltpu.VMEM((PAIR, rows), F32),
            pltpu.VMEM((PAIR, rows), F32),
            pltpu.VMEM((2 * SPAN, 2 * SPAN), BF16),
            pltpu.VMEM((2 * SPAN, 2 * SPAN), BF16),
            pltpu.VMEM((2, ext, PAIR), F32),
        ],
        compiler_params=pltpu.CompilerParams(
            dimension_semantics=("arbitrary",), vmem_limit_bytes=24 << 20
        ),
        cost_estimate=hint(9.4),
    )(pos, projected, projected, projected, grad_attn)


def order_of(count):
    if count < 4 or count & (count - 1):
        raise ValueError("context size")
    far = count // 4
    return [4 * k + 2 * y + c for c in range(2) for y in range(2) for k in range(far)]


def stacked(parts):
    rows = [p.shape[0] for p in parts]

    def body(*refs):
        out_ref, sem = refs[-2:]
        copies = [
            pltpu.make_async_copy(
                ref, out_ref.at[sum(rows[:i]) : sum(rows[: i + 1]), :], sem.at[i]
            )
            for i, ref in enumerate(refs[:-2])
        ]
        for copy in copies:
            copy.start()
        for copy in copies:
            copy.wait()

    anywhere = pl.BlockSpec(memory_space=pl.ANY)
    return pl.pallas_call(
        body,
        in_specs=[anywhere] * len(parts),
        out_specs=pl.BlockSpec(memory_space=pltpu.VMEM),
        out_shape=jax.ShapeDtypeStruct((sum(rows), parts[0].shape[1]), parts[0].dtype),
        scratch_shapes=[pltpu.SemaphoreType.DMA((len(parts),))],
        compiler_params=pltpu.CompilerParams(vmem_limit_bytes=12 << 20),
        cost_estimate=hint(1.5),
    )(*parts)


def put_in_order(out_ref, flat_ref, turned_ref, value, here, order):
    rows = turned_ref.shape[0] // len(order)
    turned_ref[...] = value.T
    for j, offset in enumerate(order):
        source = pl.multiple_of((here ^ offset) * rows, rows)
        out_ref[j * rows : (j + 1) * rows, :] = turned_ref[pl.ds(source, rows), :]
    flat_ref[...] = out_ref[...].T


def prepare(me, encoded, cotangent, order):
    frames, width = encoded.shape

    def body(me_ref, own_ref, cot_ref, x_ref, c_ref, xt_ref, ct_ref, turned_ref):
        here = me_ref[0]
        normed = normalize_values(own_ref[...].astype(F32))[0].astype(BF16)
        put_in_order(xt_ref, x_ref, turned_ref, normed, here, order)
        put_in_order(ct_ref, c_ref, turned_ref, cot_ref[...], here, order)

    sd = jax.ShapeDtypeStruct
    flat = pl.BlockSpec((SPAN, width), lambda i: (i, 0))
    turned = pl.BlockSpec((width, SPAN), lambda i: (0, i))
    return pl.pallas_call(
        body,
        grid=(frames // SPAN,),
        in_specs=[pl.BlockSpec(memory_space=pltpu.SMEM), flat, flat],
        out_specs=[pl.BlockSpec((SPAN, width), lambda i: (i + 1, 0)), flat, turned, turned],
        out_shape=[
            sd((frames + SPAN, width), BF16),
            sd((frames, width), BF16),
            sd((width, frames), BF16),
            sd((width, frames), BF16),
        ],
        scratch_shapes=[pltpu.VMEM((width, SPAN), BF16)],
        compiler_params=pltpu.CompilerParams(
            dimension_semantics=("arbitrary",), vmem_limit_bytes=24 << 20
        ),
        cost_estimate=hint(6.4),
    )(me, encoded, cotangent)


def prepare_left(me, left, x, order):
    width = left.shape[1]

    def body(me_ref, left_ref, x_ref, out_ref, ordered_ref, turned_ref):
        normed = normalize_values(left_ref[...].astype(F32))[0].astype(BF16)
        put_in_order(ordered_ref, out_ref, turned_ref, normed, me_ref[0], order)

    return pl.pallas_call(
        body,
        grid=(1,),
        in_specs=[
            pl.BlockSpec(memory_space=pltpu.SMEM),
            pl.BlockSpec((SPAN, width), lambda i: (0, 0)),
            pl.BlockSpec(memory_space=pl.ANY),
        ],
        out_specs=pl.BlockSpec((SPAN, width), lambda i: (0, 0)),
        out_shape=jax.ShapeDtypeStruct(x.shape, x.dtype),
        input_output_aliases={2: 0},
        scratch_shapes=[pltpu.VMEM((width, SPAN), BF16), pltpu.VMEM((width, SPAN), BF16)],
        compiler_params=pltpu.CompilerParams(vmem_limit_bytes=12 << 20),
        cost_estimate=hint(2.0),
    )(me, left, x)


def gradients_body(
    xt_ref, ct_ref, query_ref, main_ref, tail_ref, returned_ref, mixed_ref, keep_ref, send_ref, back_ref
):
    step = pl.program_id(0)
    half = pl.num_programs(0) // 2
    rows, cols = query_ref.shape

    @pl.when(step == 0)
    def _():
        back_ref[:, :cols] = query_ref[...]
        for i in range(2):
            part = slice((i + 1) * cols, (i + 2) * cols)
            back_ref[: rows - SPAN, part] = main_ref[i]
            back_ref[rows - SPAN :, part] = (tail_ref[i] + returned_ref[i].astype(F32)).astype(BF16)

    inner = dot_nn(xt_ref[...], back_ref[...]).astype(BF16)
    outer = dot_nn(ct_ref[...], mixed_ref[...]).astype(BF16)

    @pl.when(step < half)
    def _():
        keep_ref[:, : 3 * cols] = inner
        keep_ref[:, 3 * cols :] = outer

    @pl.when(step >= half)
    def _():
        send_ref[:, : 3 * cols] = inner
        send_ref[:, 3 * cols :] = outer


def gradients(xt, ct, query_back, main, tail, returned, mixed):
    width = xt.shape[0]
    rows, cols = mixed.shape
    tile = 256
    steps = width // tile
    whole = lambda a: pl.BlockSpec(a.shape, lambda i: (0,) * a.ndim)
    sd = jax.ShapeDtypeStruct
    return pl.pallas_call(
        gradients_body,
        grid=(steps,),
        in_specs=[
            pl.BlockSpec((tile, rows), lambda i: (i, 0)),
            pl.BlockSpec((tile, rows), lambda i: (i, 0)),
            *(whole(a) for a in (query_back, main, tail, returned, mixed)),
        ],
        out_specs=[
            pl.BlockSpec((tile, 4 * cols), lambda i: (jnp.minimum(i, steps // 2 - 1), 0)),
            pl.BlockSpec((tile, 4 * cols), lambda i: (jnp.maximum(i - steps // 2, 0), 0)),
            pl.BlockSpec((rows, 3 * cols), lambda i: (0, 0)),
        ],
        out_shape=[
            sd((width // 2, 4 * cols), BF16),
            sd((width // 2, 4 * cols), BF16),
            sd((rows, 3 * cols), BF16),
        ],
        compiler_params=pltpu.CompilerParams(
            dimension_semantics=("arbitrary",), vmem_limit_bytes=24 << 20
        ),
        cost_estimate=hint(4.0),
    )(xt, ct, query_back, main, tail, returned, mixed)


def fetch(me_ref, weight_refs, held_ref, sem, parts, count):
    here = me_ref[0]
    rows = held_ref.shape[0] // count
    copies = []
    for d in range(count):
        apart = here ^ d
        j = apart % 2 * (count // 2) + apart // 2 % 2 * (count // 4) + apart // 4
        source = pl.multiple_of(j * rows, rows)
        for g, (weight_ref, (first, cols, to)) in enumerate(zip(weight_refs, parts)):
            copies.append(
                pltpu.make_async_copy(
                    weight_ref.at[pl.ds(source, rows), first : first + cols],
                    held_ref.at[d * rows : (d + 1) * rows, to : to + cols],
                    sem.at[g, d],
                )
            )
    for copy in copies:
        copy.start()
    return copies


def finish_out(me, encoded, attended, weights, count):
    frames, width = encoded.shape
    groups = len(weights)
    parts = [(3 * w, w, first) for w, first in zip(WIDTHS, STARTS)]
    tile = 256

    def body(me_ref, enc_ref, *refs):
        mixed_refs = refs[:groups]
        weight_refs = refs[groups : 2 * groups]
        out_ref, held_ref, sem = refs[2 * groups :]
        for copy in fetch(me_ref, weight_refs, held_ref, sem, parts, count):
            copy.wait()

        def one_tile(t, carry):
            part = pl.ds(pl.multiple_of(t * tile, tile), tile)
            projected = enc_ref[:, part].astype(F32)
            for mixed_ref, (_, w, first) in zip(mixed_refs, parts):
                projected = projected + dot_nt(mixed_ref[...], held_ref[part, first : first + w])
            out_ref[:, part] = projected.astype(BF16)
            return carry

        lax.fori_loop(0, width // tile, one_tile, 0)

    vmem = pl.BlockSpec(memory_space=pltpu.VMEM)
    return pl.pallas_call(
        body,
        in_specs=[
            pl.BlockSpec(memory_space=pltpu.SMEM),
            *(vmem for _ in range(1 + groups)),
            *(pl.BlockSpec(memory_space=pl.ANY) for _ in range(groups)),
        ],
        out_specs=vmem,
        out_shape=jax.ShapeDtypeStruct((frames, width), BF16),
        scratch_shapes=[
            pltpu.VMEM((width, E), BF16),
            pltpu.SemaphoreType.DMA((groups, count)),
        ],
        compiler_params=pltpu.CompilerParams(vmem_limit_bytes=24 << 20),
        cost_estimate=hint(7.0),
    )(me, encoded, *attended, *weights)


def finish_grad(me, encoded, cotangent, backs, weights, count):
    frames, width = encoded.shape
    groups = len(weights)
    parts = [(0, 3 * w, 3 * first) for w, first in zip(WIDTHS, STARTS)]
    tile = 256

    def body(me_ref, enc_ref, cot_ref, *refs):
        back_refs = refs[:groups]
        weight_refs = refs[groups : 2 * groups]
        grad_ref, held_ref, feature_ref, sem = refs[2 * groups :]
        for copy in fetch(me_ref, weight_refs, held_ref, sem, parts, count):
            copy.wait()

        def one_tile(t, carry):
            part = pl.ds(pl.multiple_of(t * tile, tile), tile)
            feature_ref[:, part] = sum(
                dot_nt(back_ref[...], held_ref[part, first : first + w])
                for back_ref, (_, w, first) in zip(back_refs, parts)
            )
            return carry

        lax.fori_loop(0, width // tile, one_tile, 0)

        def some_rows(r, carry):
            part = pl.ds(pl.multiple_of(r * 64, 64), 64)
            unit_rows, inverse = normalize_values(enc_ref[part, :].astype(F32))
            feature = feature_ref[part, :]
            centered_grad = (
                feature
                - jnp.mean(feature, axis=1, keepdims=True)
                - unit_rows * jnp.mean(feature * unit_rows, axis=1, keepdims=True)
            )
            grad_ref[part, :] = (cot_ref[part, :].astype(F32) + inverse * centered_grad).astype(BF16)
            return carry

        lax.fori_loop(0, frames // 64, some_rows, 0)

    vmem = pl.BlockSpec(memory_space=pltpu.VMEM)
    return pl.pallas_call(
        body,
        in_specs=[
            pl.BlockSpec(memory_space=pltpu.SMEM),
            *(vmem for _ in range(2 + groups)),
            *(pl.BlockSpec(memory_space=pl.ANY) for _ in range(groups)),
        ],
        out_specs=vmem,
        out_shape=jax.ShapeDtypeStruct((frames, width), BF16),
        scratch_shapes=[
            pltpu.VMEM((width, 3 * E), BF16),
            pltpu.VMEM((frames, width), F32),
            pltpu.SemaphoreType.DMA((groups, count)),
        ],
        compiler_params=pltpu.CompilerParams(vmem_limit_bytes=36 << 20),
        cost_estimate=hint(14.0),
    )(me, encoded, cotangent, *backs, *weights)


def collect(sums):
    rows = sums[0][0].shape[0]

    def body(*refs):
        outs = refs[-4:]
        at = 0
        for (_, parts), cols, first in zip(sums, WIDTHS, STARTS):
            total = refs[at][...]
            for part_ref in refs[at + 1 : at + 1 + len(parts)]:
                total = total + part_ref[...].astype(F32)
            at += 1 + len(parts)
            for k in range(4):
                outs[k][:, first : first + cols] = total[:, k * cols : (k + 1) * cols]

    flat = [a for own, parts in sums for a in (own, *parts)]
    vmem = pl.BlockSpec(memory_space=pltpu.VMEM)
    return pl.pallas_call(
        body,
        in_specs=[vmem] * len(flat),
        out_specs=[vmem] * 4,
        out_shape=[jax.ShapeDtypeStruct((rows, E), F32)] * 4,
        compiler_params=pltpu.CompilerParams(vmem_limit_bytes=16 << 20),
        cost_estimate=hint(1.2),
    )(*flat)


def shards(encoded, query_weight, key_weight, value_weight, out_weight, cotangent, valid_frames):
    valid_count = valid_frames[0]
    frames_dev = encoded.shape[0]
    count = lax.axis_size("context")
    far = count // 4
    order = order_of(count)
    index = lax.axis_index("context").astype(jnp.int32)
    first_row = index * frames_dev
    me = index[None]
    pos = jnp.stack([first_row, valid_count])
    row_mask = (first_row + jnp.arange(frames_dev, dtype=jnp.int32) < valid_count).astype(F32)[
        :, None
    ]
    left = passed_along(encoded[frames_dev - SPAN :], "context", 1)
    sources = (query_weight, key_weight, value_weight, out_weight)

    def block_of(i, sources):
        part = slice(STARTS[i], STARTS[i] + WIDTHS[i])
        return jnp.concatenate([w[:, part] for w in sources], axis=1)

    raw, near, other, weights = ([None] * GROUPS for _ in range(4))

    def gather_far(i, *gate):
        block = block_of(i, lax.optimization_barrier((*sources, *gate))[:4] if gate else sources)
        raw[i] = (block, *(swapped(block, 4 * k) for k in range(1, far)))

    def join_far(i, *gate):
        parts = after(raw[i], *gate) if gate else raw[i]
        near[i] = stacked(parts)

    def gather_next(i, *gate):
        if gate:
            near[i] = after(near[i], *gate)
        other[i] = swapped(near[i], 2)

    def gather_chip(i, *gate):
        if gate:
            other[i] = after(other[i], *gate)
        mine = stacked([near[i], other[i]])
        weights[i] = stacked([mine, swapped(mine, 1)])

    own_x, c, xt, ct = prepare(me, encoded, cotangent, order)
    gather_far(0)
    join_far(0, own_x)
    gather_next(0)
    near_sibling = swapped(near[0], 1)
    gather_far(1, near[0])
    join_far(1)
    other[0] = after(other[0], near[1], left)
    weights[0] = stacked([near[0], other[0], near_sibling, swapped(other[0], 1)])
    x = prepare_left(me, left, own_x, order)
    gather_next(1, other[0])
    gather_far(2, near[1], other[0])

    def project(i, *gate):
        whole = after(weights[i], *gate) if gate else weights[i]
        cols = WIDTHS[i]
        projected = jnp.dot(x, whole[:, : 3 * cols], preferred_element_type=F32).astype(BF16)
        grad_attn = jnp.dot(c, whole[:, 3 * cols :], preferred_element_type=F32)
        return projected, (grad_attn * row_mask).astype(BF16)

    attended, backs, keeps, sends, sums = [], [], [], [], []

    def sum_chip(i):
        total = keeps[i].astype(F32) + swapped(sends[i], 1).astype(F32)
        half = total.shape[0] // 2
        return total[:half], total[half:].astype(BF16)

    def split_far(held, got):
        total = held + got.astype(F32)
        rows = total.shape[0] // far
        return total[:rows], [total[k * rows : (k + 1) * rows].astype(BF16) for k in range(1, far)]

    held = got = own = parts = None
    for i in range(GROUPS):
        projected, grad_attn = project(i, *((keeps[i - 1], *other[i + 1 : i + 2]) if i else ()))
        if i:
            held, send = sum_chip(i - 1)
            held, send, projected = lax.optimization_barrier((held, send, projected))
            got = swapped(send, 2)
        if i > 1:
            parts, projected = lax.optimization_barrier((parts, projected))
            sums.append((own, parts))
        mixed, query_back, main, tail, halo = attention(pos, projected, grad_attn)
        attended.append(mixed)
        returned = passed_along(halo, "context", -1)
        if i + 1 < GROUPS:
            if i + 2 < GROUPS:
                join_far(i + 2, mixed)
            gather_chip(i + 1, mixed, *(near[i + 2 : i + 3]))
        if i + 2 < GROUPS:
            gather_next(i + 2, mixed, other[i + 1])
        if i:
            held, got, mixed = lax.optimization_barrier((held, got, mixed))
            own, away = split_far(held, got)
            parts = [swapped(part, 4 * k) for k, part in enumerate(away, 1)]
        keep, send, back = gradients(xt, ct, query_back, main, tail, returned, mixed)
        keeps.append(keep)
        sends.append(send)
        backs.append(back)
    held, send = sum_chip(GROUPS - 1)
    held, send, ready = lax.optimization_barrier((held, send, me))
    got = swapped(send, 2)
    layer_out = finish_out(ready, encoded, attended, weights, count)
    got, parts, layer_out = lax.optimization_barrier((got, parts, layer_out))
    sums.append((own, parts))
    own, away = split_far(held, got)
    *away, ready = lax.optimization_barrier((*away, me))
    parts = [swapped(part, 4 * k) for k, part in enumerate(away, 1)]
    encoded_grad = finish_grad(ready, encoded, cotangent, backs, weights, count)
    parts, encoded_grad = lax.optimization_barrier((parts, encoded_grad))
    sums.append((own, parts))
    return (layer_out, encoded_grad, *collect(sums))


def solution(mesh):
    placed = (
        P(("groups", "context"), None),
        P("context", None),
        P("context", None),
        P("context", None),
        P("context", None),
        P(("groups", "context"), None),
        P("groups"),
    )
    return jax.shard_map(
        shards,
        mesh=mesh,
        in_specs=placed,
        out_specs=(P(("groups", "context"), None),) * 6,
        check_vma=False,
    )
```

```python
import jax
import jax.numpy as jnp
from jax import lax
from jax.experimental import pallas as pl
from jax.experimental.pallas import tpu as pltpu
from jax.sharding import PartitionSpec as P

HEADS = 12
HD = 64
BLOCK = 16
LEFT = 16
E = 768
SPAN = LEFT * BLOCK
HALF = SPAN // 2
PAIR = 2 * HD
SIZES = (4, 4, 4)
GROUPS = len(SIZES)
WIDTHS = tuple(HD * size for size in SIZES)
STARTS = tuple(sum(WIDTHS[:i]) for i in range(GROUPS))

epsilon = 1e-05

F32 = jnp.float32
BF16 = jnp.bfloat16

SCALE = 0.3


def hint(us):
    return pl.CostEstimate(flops=int(SCALE * us * 1.15e9), transcendentals=0, bytes_accessed=1 << 10)


def passed_along(value, axis, by):
    count = lax.axis_size(axis)
    pairs = [(i, i + by) for i in range(count) if 0 <= i + by < count]
    return lax.ppermute(value, axis, pairs)


def swapped(value, mask):
    count = lax.axis_size("context")
    return lax.ppermute(value, "context", [(i, i ^ mask) for i in range(count)])


def after(value, *others):
    return lax.optimization_barrier((value, *others))[0]


def normalize_values(values):
    centered = values - jnp.mean(values, axis=1, keepdims=True)
    inverse = lax.rsqrt(jnp.mean(centered * centered, axis=1, keepdims=True) + epsilon)
    return (centered * inverse, inverse)


def dot_nt(a, b):
    return lax.dot_general(a, b, (((1,), (1,)), ((), ())), preferred_element_type=F32)


def dot_nn(a, b):
    return lax.dot_general(a, b, (((1,), (0,)), ((), ())), preferred_element_type=F32)


def attention_body(
    pos_ref,
    q_ref,
    k_ref,
    v_ref,
    g_ref,
    o_ref,
    dq_ref,
    main_ref,
    tail_ref,
    halo_ref,
    bias_ref,
    kt_ref,
    vt_ref,
    ot_ref,
    dqt_ref,
    p_ref,
    ds_ref,
    acc_ref,
):
    rows = g_ref.shape[0]
    tiles = rows // SPAN
    first = pos_ref[0]
    count = pos_ref[1]

    @pl.when(pl.program_id(0) == 0)
    def _():
        for t in range(tiles):
            for c in range(2):
                key = lax.broadcasted_iota(jnp.int32, (SPAN + HALF, HALF), 0) + c * HALF
                query = lax.broadcasted_iota(jnp.int32, (SPAN + HALF, HALF), 1) + c * HALF
                key_block = key // BLOCK
                query_block = query // BLOCK
                pos = key + (first + (t - 1) * SPAN)
                allowed = (
                    (key_block >= query_block)
                    & (key_block <= query_block + LEFT)
                    & (pos >= 0)
                    & (pos < count)
                )
                bias_ref[t, c] = jnp.where(allowed, 0.0, -1e30)
        p_ref[...] = jnp.zeros_like(p_ref)
        ds_ref[...] = jnp.zeros_like(ds_ref)

    kt_ref[...] = k_ref[...].T
    vt_ref[...] = v_ref[...].T
    lane = lax.broadcasted_iota(jnp.int32, (SPAN, PAIR), 1)
    acc_ref[...] = jnp.zeros_like(acc_ref)

    def one_tile(t, carry):
        start = pl.multiple_of(t * SPAN, SPAN)
        qs = pl.ds(start, SPAN)
        ks = pl.ds(start, 2 * SPAN)
        q = q_ref[pl.ds(start + SPAN, SPAN), :] * BF16(HD ** (-0.5))
        g = g_ref[qs, :]
        k = k_ref[ks, :]
        v = v_ref[ks, :]
        q_heads = []
        g_heads = []
        for h in range(2):
            mine = (lane >= HD) if h else (lane < HD)
            q_heads.append(jnp.where(mine, q, jnp.zeros_like(q)))
            g_heads.append(jnp.where(mine, g, jnp.zeros_like(g)))
            s = dot_nt(k, q_heads[h])
            d = dot_nt(v, g_heads[h])
            for c in range(2):
                kr = slice(c * HALF, c * HALF + SPAN + HALF)
                qc = slice(c * HALF, (c + 1) * HALF)
                out = slice(h * SPAN + c * HALF, h * SPAN + (c + 1) * HALF)
                scores = s[kr, qc] + bias_ref[t, c]
                shifted = jnp.exp(scores - jnp.max(scores, axis=0, keepdims=True))
                probs = shifted * (1.0 / jnp.sum(shifted, axis=0, keepdims=True))
                weighted = probs * d[kr, qc]
                delta = jnp.sum(weighted, axis=0, keepdims=True)
                p_ref[kr, out] = probs.astype(BF16)
                ds_ref[kr, out] = (weighted - probs * delta).astype(BF16)
            hs = slice(h * HD, (h + 1) * HD)
            cols = slice(h * SPAN, (h + 1) * SPAN)
            ot_ref[hs, qs] = dot_nn(vt_ref[hs, ks], p_ref[:, cols])
            dqt_ref[hs, qs] = dot_nn(kt_ref[hs, ks], ds_ref[:, cols]) * HD ** (-0.5)
        acc_ref[0, ks, :] += dot_nn(ds_ref[...], jnp.concatenate(q_heads, axis=0))
        acc_ref[1, ks, :] += dot_nn(p_ref[...], jnp.concatenate(g_heads, axis=0))
        return carry

    lax.fori_loop(0, tiles, one_tile, 0, unroll=True)
    row = lax.broadcasted_iota(jnp.int32, (rows, PAIR), 0) + first
    o_ref[...] = jnp.where(row < count, ot_ref[...].T, 0.0).astype(BF16)
    dq_ref[...] = dqt_ref[...].T.astype(BF16)
    halo_ref[...] = acc_ref[:, :SPAN, :].astype(BF16)
    main_ref[...] = acc_ref[:, SPAN:rows, :].astype(BF16)
    tail_ref[...] = acc_ref[:, rows:, :]


def attention(pos, projected, grad_attn):
    rows, cols = grad_attn.shape
    ext = rows + SPAN
    steps = cols // PAIR
    sd = jax.ShapeDtypeStruct
    column = lambda part: pl.BlockSpec((ext, PAIR), lambda j: (0, part * steps + j))
    flat = pl.BlockSpec((rows, PAIR), lambda j: (0, j))
    both = lambda r: pl.BlockSpec((2, r, PAIR), lambda j: (0, 0, j))
    return pl.pallas_call(
        attention_body,
        grid=(steps,),
        in_specs=[pl.BlockSpec(memory_space=pltpu.SMEM), column(0), column(1), column(2), flat],
        out_specs=[flat, flat, both(rows - SPAN), both(SPAN), both(SPAN)],
        out_shape=[
            sd((rows, cols), BF16),
            sd((rows, cols), BF16),
            sd((2, rows - SPAN, cols), BF16),
            sd((2, SPAN, cols), F32),
            sd((2, SPAN, cols), BF16),
        ],
        scratch_shapes=[
            pltpu.VMEM((rows // SPAN, 2, SPAN + HALF, HALF), F32),
            pltpu.VMEM((PAIR, ext), BF16),
            pltpu.VMEM((PAIR, ext), BF16),
            pltpu.VMEM((PAIR, rows), F32),
            pltpu.VMEM((PAIR, rows), F32),
            pltpu.VMEM((2 * SPAN, 2 * SPAN), BF16),
            pltpu.VMEM((2 * SPAN, 2 * SPAN), BF16),
            pltpu.VMEM((2, ext, PAIR), F32),
        ],
        compiler_params=pltpu.CompilerParams(
            dimension_semantics=("arbitrary",), vmem_limit_bytes=24 << 20
        ),
        cost_estimate=hint(9.4),
    )(pos, projected, projected, projected, grad_attn)


def order_of(count):
    if count < 4 or count & (count - 1):
        raise ValueError("context size")
    far = count // 4
    return [4 * k + 2 * y + c for c in range(2) for y in range(2) for k in range(far)]


def joined(parts, shape, sources, targets, grant=12):
    def body(*refs):
        out_ref, sem = refs[-2:]
        copies = [
            pltpu.make_async_copy(ref.at[source], out_ref.at[target], sem.at[i])
            for i, (ref, source, target) in enumerate(zip(refs[:-2], sources, targets))
        ]
        for copy in copies:
            copy.start()
        for copy in copies:
            copy.wait()

    return pl.pallas_call(
        body,
        in_specs=[pl.BlockSpec(memory_space=pltpu.HBM)] * len(parts),
        out_specs=pl.BlockSpec(memory_space=pltpu.VMEM),
        out_shape=jax.ShapeDtypeStruct(shape, parts[0].dtype),
        scratch_shapes=[pltpu.SemaphoreType.DMA((len(parts),))],
        compiler_params=pltpu.CompilerParams(vmem_limit_bytes=grant << 20),
        cost_estimate=hint(1.5),
    )(*parts)


def stacked(parts):
    ends = [sum(p.shape[0] for p in parts[: i + 1]) for i in range(len(parts))]
    whole = [(slice(None), slice(None))] * len(parts)
    targets = [(slice(end - p.shape[0], end), slice(None)) for end, p in zip(ends, parts)]
    return joined(parts, (ends[-1], parts[0].shape[1]), whole, targets)


def put_in_order(out_ref, flat_ref, turned_ref, value, here, order):
    rows = turned_ref.shape[0] // len(order)
    turned_ref[...] = value.T
    for j, offset in enumerate(order):
        source = pl.multiple_of((here ^ offset) * rows, rows)
        out_ref[j * rows : (j + 1) * rows, :] = turned_ref[pl.ds(source, rows), :]
    flat_ref[...] = out_ref[...].T


def prepare(me, encoded, cotangent, order):
    frames, width = encoded.shape

    def body(me_ref, own_ref, cot_ref, x_ref, c_ref, xt_ref, ct_ref, turned_ref):
        here = me_ref[0]
        normed = normalize_values(own_ref[...].astype(F32))[0].astype(BF16)
        put_in_order(xt_ref, x_ref, turned_ref, normed, here, order)
        put_in_order(ct_ref, c_ref, turned_ref, cot_ref[...], here, order)

    sd = jax.ShapeDtypeStruct
    flat = pl.BlockSpec((SPAN, width), lambda i: (i, 0))
    turned = pl.BlockSpec((width, SPAN), lambda i: (0, i))
    return pl.pallas_call(
        body,
        grid=(frames // SPAN,),
        in_specs=[pl.BlockSpec(memory_space=pltpu.SMEM), flat, flat],
        out_specs=[pl.BlockSpec((SPAN, width), lambda i: (i + 1, 0)), flat, turned, turned],
        out_shape=[
            sd((frames + SPAN, width), BF16),
            sd((frames, width), BF16),
            sd((width, frames), BF16),
            sd((width, frames), BF16),
        ],
        scratch_shapes=[pltpu.VMEM((width, SPAN), BF16)],
        compiler_params=pltpu.CompilerParams(
            dimension_semantics=("arbitrary",), vmem_limit_bytes=60 << 20
        ),
        cost_estimate=hint(6.4),
    )(me, encoded, cotangent)


def prepare_left(me, left, x, order):
    width = left.shape[1]

    def body(me_ref, left_ref, x_ref, out_ref, ordered_ref, turned_ref):
        normed = normalize_values(left_ref[...].astype(F32))[0].astype(BF16)
        put_in_order(ordered_ref, out_ref, turned_ref, normed, me_ref[0], order)

    return pl.pallas_call(
        body,
        grid=(1,),
        in_specs=[
            pl.BlockSpec(memory_space=pltpu.SMEM),
            pl.BlockSpec((SPAN, width), lambda i: (0, 0)),
            pl.BlockSpec(memory_space=pl.ANY),
        ],
        out_specs=pl.BlockSpec((SPAN, width), lambda i: (0, 0)),
        out_shape=jax.ShapeDtypeStruct(x.shape, x.dtype),
        input_output_aliases={2: 0},
        scratch_shapes=[pltpu.VMEM((width, SPAN), BF16), pltpu.VMEM((width, SPAN), BF16)],
        compiler_params=pltpu.CompilerParams(vmem_limit_bytes=12 << 20),
        cost_estimate=hint(2.0),
    )(me, left, x)


def gradients_body(
    xt_ref, ct_ref, query_ref, main_ref, tail_ref, returned_ref, mixed_ref, keep_ref, send_ref, back_ref
):
    step = pl.program_id(0)
    half = pl.num_programs(0) // 2
    rows, cols = query_ref.shape

    @pl.when(step == 0)
    def _():
        back_ref[:, :cols] = query_ref[...]
        for i in range(2):
            part = slice((i + 1) * cols, (i + 2) * cols)
            back_ref[: rows - SPAN, part] = main_ref[i]
            back_ref[rows - SPAN :, part] = (tail_ref[i] + returned_ref[i].astype(F32)).astype(BF16)

    inner = dot_nn(xt_ref[...], back_ref[...]).astype(BF16)
    outer = dot_nn(ct_ref[...], mixed_ref[...]).astype(BF16)

    @pl.when(step < half)
    def _():
        keep_ref[:, : 3 * cols] = inner
        keep_ref[:, 3 * cols :] = outer

    @pl.when(step >= half)
    def _():
        send_ref[:, : 3 * cols] = inner
        send_ref[:, 3 * cols :] = outer


def gradients(xt, ct, query_back, main, tail, returned, mixed, us):
    width = xt.shape[0]
    rows, cols = mixed.shape
    tile = 256
    steps = width // tile
    whole = lambda a: pl.BlockSpec(a.shape, lambda i: (0,) * a.ndim)
    sd = jax.ShapeDtypeStruct
    return pl.pallas_call(
        gradients_body,
        grid=(steps,),
        in_specs=[
            pl.BlockSpec((tile, rows), lambda i: (i, 0)),
            pl.BlockSpec((tile, rows), lambda i: (i, 0)),
            *(whole(a) for a in (query_back, main, tail, returned, mixed)),
        ],
        out_specs=[
            pl.BlockSpec((tile, 4 * cols), lambda i: (jnp.minimum(i, steps // 2 - 1), 0)),
            pl.BlockSpec((tile, 4 * cols), lambda i: (jnp.maximum(i - steps // 2, 0), 0)),
            pl.BlockSpec((rows, 3 * cols), lambda i: (0, 0)),
        ],
        out_shape=[
            sd((width // 2, 4 * cols), BF16),
            sd((width // 2, 4 * cols), BF16),
            sd((rows, 3 * cols), BF16),
        ],
        compiler_params=pltpu.CompilerParams(
            dimension_semantics=("arbitrary",), vmem_limit_bytes=24 << 20
        ),
        cost_estimate=hint(us),
    )(xt, ct, query_back, main, tail, returned, mixed)


def fetch(me_ref, weight_refs, held_ref, sem, parts, count):
    here = me_ref[0]
    rows = held_ref.shape[0] // count
    copies = []
    for d in range(count):
        apart = here ^ d
        j = apart % 2 * (count // 2) + apart // 2 % 2 * (count // 4) + apart // 4
        source = pl.multiple_of(j * rows, rows)
        for g, (weight_ref, (first, cols, to)) in enumerate(zip(weight_refs, parts)):
            copies.append(
                pltpu.make_async_copy(
                    weight_ref.at[pl.ds(source, rows), first : first + cols],
                    held_ref.at[d * rows : (d + 1) * rows, to : to + cols],
                    sem.at[g, d],
                )
            )
    for copy in copies:
        copy.start()
    return copies


def finish_out(me, encoded, attended, weights, count):
    frames, width = encoded.shape
    groups = len(weights)
    parts = [(3 * w, w, first) for w, first in zip(WIDTHS, STARTS)]
    tile = 256

    def body(me_ref, enc_ref, *refs):
        mixed_refs = refs[:groups]
        weight_refs = refs[groups : 2 * groups]
        out_ref, held_ref, sem = refs[2 * groups :]
        for copy in fetch(me_ref, weight_refs, held_ref, sem, parts, count):
            copy.wait()

        def one_tile(t, carry):
            part = pl.ds(pl.multiple_of(t * tile, tile), tile)
            projected = enc_ref[:, part].astype(F32)
            for mixed_ref, (_, w, first) in zip(mixed_refs, parts):
                projected = projected + dot_nt(mixed_ref[...], held_ref[part, first : first + w])
            out_ref[:, part] = projected.astype(BF16)
            return carry

        lax.fori_loop(0, width // tile, one_tile, 0)

    vmem = pl.BlockSpec(memory_space=pltpu.VMEM)
    return pl.pallas_call(
        body,
        in_specs=[
            pl.BlockSpec(memory_space=pltpu.SMEM),
            *(vmem for _ in range(1 + groups)),
            *(pl.BlockSpec(memory_space=pl.ANY) for _ in range(groups)),
        ],
        out_specs=vmem,
        out_shape=jax.ShapeDtypeStruct((frames, width), BF16),
        scratch_shapes=[
            pltpu.VMEM((width, E), BF16),
            pltpu.SemaphoreType.DMA((groups, count)),
        ],
        compiler_params=pltpu.CompilerParams(vmem_limit_bytes=24 << 20),
        cost_estimate=hint(0.1),
    )(me, encoded, *attended, *weights)


def finish_grad(me, encoded, cotangent, backs, weights, count):
    frames, width = encoded.shape
    groups = len(weights)
    parts = [(0, 3 * w, 3 * first) for w, first in zip(WIDTHS, STARTS)]
    tile = 256

    def body(me_ref, enc_ref, cot_ref, *refs):
        back_refs = refs[:groups]
        weight_refs = refs[groups : 2 * groups]
        grad_ref, held_ref, feature_ref, sem = refs[2 * groups :]
        for copy in fetch(me_ref, weight_refs, held_ref, sem, parts, count):
            copy.wait()

        def one_tile(t, carry):
            part = pl.ds(pl.multiple_of(t * tile, tile), tile)
            feature_ref[:, part] = sum(
                dot_nt(back_ref[...], held_ref[part, first : first + w])
                for back_ref, (_, w, first) in zip(back_refs, parts)
            )
            return carry

        lax.fori_loop(0, width // tile, one_tile, 0)

        def some_rows(r, carry):
            part = pl.ds(pl.multiple_of(r * 64, 64), 64)
            unit_rows, inverse = normalize_values(enc_ref[part, :].astype(F32))
            feature = feature_ref[part, :]
            centered_grad = (
                feature
                - jnp.mean(feature, axis=1, keepdims=True)
                - unit_rows * jnp.mean(feature * unit_rows, axis=1, keepdims=True)
            )
            grad_ref[part, :] = (cot_ref[part, :].astype(F32) + inverse * centered_grad).astype(BF16)
            return carry

        lax.fori_loop(0, frames // 64, some_rows, 0)

    vmem = pl.BlockSpec(memory_space=pltpu.VMEM)
    return pl.pallas_call(
        body,
        in_specs=[
            pl.BlockSpec(memory_space=pltpu.SMEM),
            *(vmem for _ in range(2 + groups)),
            *(pl.BlockSpec(memory_space=pl.ANY) for _ in range(groups)),
        ],
        out_specs=vmem,
        out_shape=jax.ShapeDtypeStruct((frames, width), BF16),
        scratch_shapes=[
            pltpu.VMEM((width, 3 * E), BF16),
            pltpu.VMEM((frames, width), F32),
            pltpu.SemaphoreType.DMA((groups, count)),
        ],
        compiler_params=pltpu.CompilerParams(vmem_limit_bytes=36 << 20),
        cost_estimate=hint(14.0),
    )(me, encoded, cotangent, *backs, *weights)


def collect(sums):
    rows = sums[0][0].shape[0]

    def body(*refs):
        outs = refs[-4:]
        at = 0
        for (_, parts), cols, first in zip(sums, WIDTHS, STARTS):
            total = refs[at][...]
            for part_ref in refs[at + 1 : at + 1 + len(parts)]:
                total = total + part_ref[...].astype(F32)
            at += 1 + len(parts)
            for k in range(4):
                outs[k][:, first : first + cols] = total[:, k * cols : (k + 1) * cols]

    flat = [a for own, parts in sums for a in (own, *parts)]
    vmem = pl.BlockSpec(memory_space=pltpu.VMEM)
    return pl.pallas_call(
        body,
        in_specs=[vmem] * len(flat),
        out_specs=[vmem] * 4,
        out_shape=[jax.ShapeDtypeStruct((rows, E), F32)] * 4,
        compiler_params=pltpu.CompilerParams(vmem_limit_bytes=16 << 20),
        cost_estimate=hint(1.2),
    )(*flat)


def shards(encoded, query_weight, key_weight, value_weight, out_weight, cotangent, valid_frames):
    valid_count = valid_frames[0]
    frames_dev = encoded.shape[0]
    count = lax.axis_size("context")
    far = count // 4
    order = order_of(count)
    index = lax.axis_index("context").astype(jnp.int32)
    first_row = index * frames_dev
    me = index[None]
    pos = jnp.stack([first_row, valid_count])
    row_mask = (first_row + jnp.arange(frames_dev, dtype=jnp.int32) < valid_count).astype(F32)[
        :, None
    ]
    left = passed_along(encoded[frames_dev - SPAN :], "context", 1)
    sources = (query_weight, key_weight, value_weight, out_weight)

    def block_of(i, sources):
        cols = WIDTHS[i]
        part = (slice(None), slice(STARTS[i], STARTS[i] + cols))
        targets = [(slice(None), slice(k * cols, (k + 1) * cols)) for k in range(4)]
        shape = (sources[0].shape[0], 4 * cols)
        return joined(sources, shape, [part] * 4, targets, 12 if i else 60)

    raw, near, other, weights = ([None] * GROUPS for _ in range(4))

    def gather_far(i, *gate):
        block = block_of(i, lax.optimization_barrier((*sources, *gate))[:4] if gate else sources)
        raw[i] = (block, *(swapped(block, 4 * k) for k in range(1, far)))

    def join_far(i, *gate):
        parts = after(raw[i], *gate) if gate else raw[i]
        near[i] = stacked(parts)

    def gather_next(i, *gate):
        if gate:
            near[i] = after(near[i], *gate)
        other[i] = swapped(near[i], 2)

    def gather_chip(i, *gate):
        if gate:
            other[i] = after(other[i], *gate)
        mine = stacked([near[i], other[i]])
        weights[i] = stacked([mine, swapped(mine, 1)])

    own_x, c, xt, ct = prepare(me, encoded, cotangent, order)
    gather_far(0)
    join_far(0, own_x)
    gather_next(0)
    near_sibling = swapped(near[0], 1)
    gather_far(1, near[0])
    join_far(1)
    other[0] = after(other[0], near[1], left)
    weights[0] = stacked([near[0], other[0], near_sibling, swapped(other[0], 1)])
    x = prepare_left(me, left, own_x, order)
    gather_next(1, other[0])
    gather_far(2, near[1], other[0])

    def project(i, *gate):
        whole = after(weights[i], *gate) if gate else weights[i]
        cols = WIDTHS[i]
        projected = jnp.dot(x, whole[:, : 3 * cols], preferred_element_type=F32).astype(BF16)
        grad_attn = jnp.dot(c, whole[:, 3 * cols :], preferred_element_type=F32)
        return projected, (grad_attn * row_mask).astype(BF16)

    attended, backs, keeps, sends, sums = [], [], [], [], []

    def sum_chip(i):
        total = keeps[i].astype(F32) + swapped(sends[i], 1).astype(F32)
        half = total.shape[0] // 2
        return total[:half], total[half:].astype(BF16)

    def split_far(held, got):
        total = held + got.astype(F32)
        rows = total.shape[0] // far
        return total[:rows], [total[k * rows : (k + 1) * rows].astype(BF16) for k in range(1, far)]

    held = got = own = parts = None
    for i in range(GROUPS):
        projected, grad_attn = project(i, *((attended[i - 1], *other[i + 1 : i + 2]) if i else ()))
        if i:
            held, send = sum_chip(i - 1)
            held, send, projected = lax.optimization_barrier((held, send, projected))
            got = swapped(send, 2)
        if i > 1:
            parts, projected = lax.optimization_barrier((parts, projected))
            sums.append((own, parts))
        mixed, query_back, main, tail, halo = attention(pos, projected, grad_attn)
        attended.append(mixed)
        returned = passed_along(halo, "context", -1)
        if i + 1 < GROUPS:
            if i + 2 < GROUPS:
                join_far(i + 2, mixed)
            gather_chip(i + 1, mixed, *(near[i + 2 : i + 3]))
        if i + 2 < GROUPS:
            gather_next(i + 2, mixed, other[i + 1])
        if i:
            held, got, mixed = lax.optimization_barrier((held, got, mixed))
            own, away = split_far(held, got)
            parts = [swapped(part, 4 * k) for k, part in enumerate(away, 1)]
        keep, send, back = gradients(
            xt, ct, query_back, main, tail, returned, mixed, 4.0 if i + 1 < GROUPS else 0.1
        )
        keeps.append(keep)
        sends.append(send)
        backs.append(back)
    held, send = sum_chip(GROUPS - 1)
    held, send, ready = lax.optimization_barrier((held, send, me))
    got = swapped(send, 2)
    layer_out = finish_out(ready, encoded, attended, weights, count)
    got, parts, layer_out = lax.optimization_barrier((got, parts, layer_out))
    sums.append((own, parts))
    own, away = split_far(held, got)
    *away, ready = lax.optimization_barrier((*away, me))
    parts = [swapped(part, 4 * k) for k, part in enumerate(away, 1)]
    encoded_grad = finish_grad(ready, encoded, cotangent, backs, weights, count)
    parts, encoded_grad = lax.optimization_barrier((parts, encoded_grad))
    sums.append((own, parts))
    return (layer_out, encoded_grad, *collect(sums))


def solution(mesh):
    placed = (
        P(("groups", "context"), None),
        P("context", None),
        P("context", None),
        P("context", None),
        P("context", None),
        P(("groups", "context"), None),
        P("groups"),
    )
    return jax.shard_map(
        shards,
        mesh=mesh,
        in_specs=placed,
        out_specs=(P(("groups", "context"), None),) * 6,
        check_vma=False,
    )
```

```python
import jax
import jax.numpy as jnp
from jax import lax
from jax.experimental import pallas as pl
from jax.experimental.pallas import tpu as pltpu
from jax.sharding import PartitionSpec as P

HEADS = 12
HD = 64
BLOCK = 16
LEFT = 16
E = 768
SPAN = LEFT * BLOCK
HALF = SPAN // 2
PAIR = 2 * HD
SIZES = (4, 4, 4)
GROUPS = len(SIZES)
WIDTHS = tuple(HD * size for size in SIZES)
STARTS = tuple(sum(WIDTHS[:i]) for i in range(GROUPS))

epsilon = 1e-05

F32 = jnp.float32
BF16 = jnp.bfloat16

SCALE = 0.3


def hint(us):
    return pl.CostEstimate(flops=int(SCALE * us * 1.15e9), transcendentals=0, bytes_accessed=1 << 10)


def passed_along(value, axis, by):
    count = lax.axis_size(axis)
    pairs = [(i, i + by) for i in range(count) if 0 <= i + by < count]
    return lax.ppermute(value, axis, pairs)


def swapped(value, mask):
    count = lax.axis_size("context")
    return lax.ppermute(value, "context", [(i, i ^ mask) for i in range(count)])


def after(value, *others):
    return lax.optimization_barrier((value, *others))[0]


def normalize_values(values):
    centered = values - jnp.mean(values, axis=1, keepdims=True)
    inverse = lax.rsqrt(jnp.mean(centered * centered, axis=1, keepdims=True) + epsilon)
    return (centered * inverse, inverse)


def dot_nt(a, b):
    return lax.dot_general(a, b, (((1,), (1,)), ((), ())), preferred_element_type=F32)


def dot_nn(a, b):
    return lax.dot_general(a, b, (((1,), (0,)), ((), ())), preferred_element_type=F32)


def attention_body(
    pos_ref,
    q_ref,
    k_ref,
    v_ref,
    g_ref,
    o_ref,
    dq_ref,
    main_ref,
    tail_ref,
    halo_ref,
    bias_ref,
    kt_ref,
    vt_ref,
    ot_ref,
    dqt_ref,
    p_ref,
    ds_ref,
    acc_ref,
):
    rows = g_ref.shape[0]
    tiles = rows // SPAN
    first = pos_ref[0]
    count = pos_ref[1]

    @pl.when(pl.program_id(0) == 0)
    def _():
        for t in range(tiles):
            for c in range(2):
                key = lax.broadcasted_iota(jnp.int32, (SPAN + HALF, HALF), 0) + c * HALF
                query = lax.broadcasted_iota(jnp.int32, (SPAN + HALF, HALF), 1) + c * HALF
                key_block = key // BLOCK
                query_block = query // BLOCK
                pos = key + (first + (t - 1) * SPAN)
                allowed = (
                    (key_block >= query_block)
                    & (key_block <= query_block + LEFT)
                    & (pos >= 0)
                    & (pos < count)
                )
                bias_ref[t, c] = jnp.where(allowed, 0.0, -1e30)
        p_ref[...] = jnp.zeros_like(p_ref)
        ds_ref[...] = jnp.zeros_like(ds_ref)

    kt_ref[...] = k_ref[...].T
    vt_ref[...] = v_ref[...].T
    lane = lax.broadcasted_iota(jnp.int32, (SPAN, PAIR), 1)
    acc_ref[...] = jnp.zeros_like(acc_ref)

    def one_tile(t, carry):
        start = pl.multiple_of(t * SPAN, SPAN)
        qs = pl.ds(start, SPAN)
        ks = pl.ds(start, 2 * SPAN)
        q = q_ref[pl.ds(start + SPAN, SPAN), :] * BF16(HD ** (-0.5))
        g = g_ref[qs, :]
        k = k_ref[ks, :]
        v = v_ref[ks, :]
        q_heads = []
        g_heads = []
        for h in range(2):
            mine = (lane >= HD) if h else (lane < HD)
            q_heads.append(jnp.where(mine, q, jnp.zeros_like(q)))
            g_heads.append(jnp.where(mine, g, jnp.zeros_like(g)))
            s = dot_nt(k, q_heads[h])
            d = dot_nt(v, g_heads[h])
            for c in range(2):
                kr = slice(c * HALF, c * HALF + SPAN + HALF)
                qc = slice(c * HALF, (c + 1) * HALF)
                out = slice(h * SPAN + c * HALF, h * SPAN + (c + 1) * HALF)
                scores = s[kr, qc] + bias_ref[t, c]
                shifted = jnp.exp(scores - jnp.max(scores, axis=0, keepdims=True))
                probs = shifted * (1.0 / jnp.sum(shifted, axis=0, keepdims=True))
                weighted = probs * d[kr, qc]
                delta = jnp.sum(weighted, axis=0, keepdims=True)
                p_ref[kr, out] = probs.astype(BF16)
                ds_ref[kr, out] = (weighted - probs * delta).astype(BF16)
            hs = slice(h * HD, (h + 1) * HD)
            cols = slice(h * SPAN, (h + 1) * SPAN)
            ot_ref[hs, qs] = dot_nn(vt_ref[hs, ks], p_ref[:, cols])
            dqt_ref[hs, qs] = dot_nn(kt_ref[hs, ks], ds_ref[:, cols]) * HD ** (-0.5)
        acc_ref[0, ks, :] += dot_nn(ds_ref[...], jnp.concatenate(q_heads, axis=0))
        acc_ref[1, ks, :] += dot_nn(p_ref[...], jnp.concatenate(g_heads, axis=0))
        return carry

    lax.fori_loop(0, tiles, one_tile, 0, unroll=True)
    row = lax.broadcasted_iota(jnp.int32, (rows, PAIR), 0) + first
    o_ref[...] = jnp.where(row < count, ot_ref[...].T, 0.0).astype(BF16)
    dq_ref[...] = dqt_ref[...].T.astype(BF16)
    halo_ref[...] = acc_ref[:, :SPAN, :].astype(BF16)
    main_ref[...] = acc_ref[:, SPAN:rows, :].astype(BF16)
    tail_ref[...] = acc_ref[:, rows:, :]


def attention(pos, projected, grad_attn):
    rows, cols = grad_attn.shape
    ext = rows + SPAN
    steps = cols // PAIR
    sd = jax.ShapeDtypeStruct
    column = lambda part: pl.BlockSpec((ext, PAIR), lambda j: (0, part * steps + j))
    flat = pl.BlockSpec((rows, PAIR), lambda j: (0, j))
    both = lambda r: pl.BlockSpec((2, r, PAIR), lambda j: (0, 0, j))
    return pl.pallas_call(
        attention_body,
        grid=(steps,),
        in_specs=[pl.BlockSpec(memory_space=pltpu.SMEM), column(0), column(1), column(2), flat],
        out_specs=[flat, flat, both(rows - SPAN), both(SPAN), both(SPAN)],
        out_shape=[
            sd((rows, cols), BF16),
            sd((rows, cols), BF16),
            sd((2, rows - SPAN, cols), BF16),
            sd((2, SPAN, cols), F32),
            sd((2, SPAN, cols), BF16),
        ],
        scratch_shapes=[
            pltpu.VMEM((rows // SPAN, 2, SPAN + HALF, HALF), F32),
            pltpu.VMEM((PAIR, ext), BF16),
            pltpu.VMEM((PAIR, ext), BF16),
            pltpu.VMEM((PAIR, rows), F32),
            pltpu.VMEM((PAIR, rows), F32),
            pltpu.VMEM((2 * SPAN, 2 * SPAN), BF16),
            pltpu.VMEM((2 * SPAN, 2 * SPAN), BF16),
            pltpu.VMEM((2, ext, PAIR), F32),
        ],
        compiler_params=pltpu.CompilerParams(
            dimension_semantics=("arbitrary",), vmem_limit_bytes=24 << 20
        ),
        cost_estimate=hint(9.4),
    )(pos, projected, projected, projected, grad_attn)


def order_of(count):
    if count < 4 or count & (count - 1):
        raise ValueError("context size")
    far = count // 4
    return [4 * k + 2 * y + c for c in range(2) for y in range(2) for k in range(far)]


def joined(parts, shape, sources, targets, grant=12):
    def body(*refs):
        out_ref, sem = refs[-2:]
        copies = [
            pltpu.make_async_copy(ref.at[source], out_ref.at[target], sem.at[i])
            for i, (ref, source, target) in enumerate(zip(refs[:-2], sources, targets))
        ]
        for copy in copies:
            copy.start()
        for copy in copies:
            copy.wait()

    return pl.pallas_call(
        body,
        in_specs=[pl.BlockSpec(memory_space=pltpu.HBM)] * len(parts),
        out_specs=pl.BlockSpec(memory_space=pltpu.VMEM),
        out_shape=jax.ShapeDtypeStruct(shape, parts[0].dtype),
        scratch_shapes=[pltpu.SemaphoreType.DMA((len(parts),))],
        compiler_params=pltpu.CompilerParams(vmem_limit_bytes=grant << 20),
        cost_estimate=hint(1.5),
    )(*parts)


def stacked(parts):
    ends = [sum(p.shape[0] for p in parts[: i + 1]) for i in range(len(parts))]
    whole = [(slice(None), slice(None))] * len(parts)
    targets = [(slice(end - p.shape[0], end), slice(None)) for end, p in zip(ends, parts)]
    return joined(parts, (ends[-1], parts[0].shape[1]), whole, targets)


def put_in_order(out_ref, flat_ref, turned_ref, value, here, order):
    rows = turned_ref.shape[0] // len(order)
    turned_ref[...] = value.T
    for j, offset in enumerate(order):
        source = pl.multiple_of((here ^ offset) * rows, rows)
        out_ref[j * rows : (j + 1) * rows, :] = turned_ref[pl.ds(source, rows), :]
    flat_ref[...] = out_ref[...].T


def prepare(me, encoded, cotangent, order):
    frames, width = encoded.shape

    def body(me_ref, own_ref, cot_ref, x_ref, c_ref, xt_ref, ct_ref, turned_ref):
        here = me_ref[0]
        normed = normalize_values(own_ref[...].astype(F32))[0].astype(BF16)
        put_in_order(xt_ref, x_ref, turned_ref, normed, here, order)
        put_in_order(ct_ref, c_ref, turned_ref, cot_ref[...], here, order)

    sd = jax.ShapeDtypeStruct
    flat = pl.BlockSpec((SPAN, width), lambda i: (i, 0))
    turned = pl.BlockSpec((width, SPAN), lambda i: (0, i))
    return pl.pallas_call(
        body,
        grid=(frames // SPAN,),
        in_specs=[pl.BlockSpec(memory_space=pltpu.SMEM), flat, flat],
        out_specs=[pl.BlockSpec((SPAN, width), lambda i: (i + 1, 0)), flat, turned, turned],
        out_shape=[
            sd((frames + SPAN, width), BF16),
            sd((frames, width), BF16),
            sd((width, frames), BF16),
            sd((width, frames), BF16),
        ],
        scratch_shapes=[pltpu.VMEM((width, SPAN), BF16)],
        compiler_params=pltpu.CompilerParams(
            dimension_semantics=("arbitrary",), vmem_limit_bytes=60 << 20
        ),
        cost_estimate=hint(6.4),
    )(me, encoded, cotangent)


def prepare_left(me, left, x, order):
    width = left.shape[1]

    def body(me_ref, left_ref, x_ref, out_ref, ordered_ref, turned_ref):
        normed = normalize_values(left_ref[...].astype(F32))[0].astype(BF16)
        put_in_order(ordered_ref, out_ref, turned_ref, normed, me_ref[0], order)

    return pl.pallas_call(
        body,
        grid=(1,),
        in_specs=[
            pl.BlockSpec(memory_space=pltpu.SMEM),
            pl.BlockSpec((SPAN, width), lambda i: (0, 0)),
            pl.BlockSpec(memory_space=pl.ANY),
        ],
        out_specs=pl.BlockSpec((SPAN, width), lambda i: (0, 0)),
        out_shape=jax.ShapeDtypeStruct(x.shape, x.dtype),
        input_output_aliases={2: 0},
        scratch_shapes=[pltpu.VMEM((width, SPAN), BF16), pltpu.VMEM((width, SPAN), BF16)],
        compiler_params=pltpu.CompilerParams(vmem_limit_bytes=12 << 20),
        cost_estimate=hint(2.0),
    )(me, left, x)


def gradients_body(
    xt_ref, ct_ref, query_ref, main_ref, tail_ref, returned_ref, mixed_ref, keep_ref, send_ref, back_ref
):
    step = pl.program_id(0)
    half = pl.num_programs(0) // 2
    rows, cols = query_ref.shape

    @pl.when(step == 0)
    def _():
        back_ref[:, :cols] = query_ref[...]
        for i in range(2):
            part = slice((i + 1) * cols, (i + 2) * cols)
            back_ref[: rows - SPAN, part] = main_ref[i]
            back_ref[rows - SPAN :, part] = (tail_ref[i] + returned_ref[i].astype(F32)).astype(BF16)

    inner = dot_nn(xt_ref[...], back_ref[...]).astype(BF16)
    outer = dot_nn(ct_ref[...], mixed_ref[...]).astype(BF16)

    @pl.when(step < half)
    def _():
        keep_ref[:, : 3 * cols] = inner
        keep_ref[:, 3 * cols :] = outer

    @pl.when(step >= half)
    def _():
        send_ref[:, : 3 * cols] = inner
        send_ref[:, 3 * cols :] = outer


def gradients(xt, ct, query_back, main, tail, returned, mixed, us):
    width = xt.shape[0]
    rows, cols = mixed.shape
    tile = 256
    steps = width // tile
    whole = lambda a: pl.BlockSpec(a.shape, lambda i: (0,) * a.ndim)
    sd = jax.ShapeDtypeStruct
    return pl.pallas_call(
        gradients_body,
        grid=(steps,),
        in_specs=[
            pl.BlockSpec((tile, rows), lambda i: (i, 0)),
            pl.BlockSpec((tile, rows), lambda i: (i, 0)),
            *(whole(a) for a in (query_back, main, tail, returned, mixed)),
        ],
        out_specs=[
            pl.BlockSpec((tile, 4 * cols), lambda i: (jnp.minimum(i, steps // 2 - 1), 0)),
            pl.BlockSpec((tile, 4 * cols), lambda i: (jnp.maximum(i - steps // 2, 0), 0)),
            pl.BlockSpec((rows, 3 * cols), lambda i: (0, 0)),
        ],
        out_shape=[
            sd((width // 2, 4 * cols), BF16),
            sd((width // 2, 4 * cols), BF16),
            sd((rows, 3 * cols), BF16),
        ],
        compiler_params=pltpu.CompilerParams(
            dimension_semantics=("arbitrary",), vmem_limit_bytes=24 << 20
        ),
        cost_estimate=hint(us),
    )(xt, ct, query_back, main, tail, returned, mixed)


def fetch(me_ref, weight_refs, held_ref, sem, parts, count):
    here = me_ref[0]
    rows = held_ref.shape[0] // count
    copies = []
    for d in range(count):
        apart = here ^ d
        j = apart % 2 * (count // 2) + apart // 2 % 2 * (count // 4) + apart // 4
        source = pl.multiple_of(j * rows, rows)
        for g, (weight_ref, (first, cols, to)) in enumerate(zip(weight_refs, parts)):
            copies.append(
                pltpu.make_async_copy(
                    weight_ref.at[pl.ds(source, rows), first : first + cols],
                    held_ref.at[d * rows : (d + 1) * rows, to : to + cols],
                    sem.at[g, d],
                )
            )
    for copy in copies:
        copy.start()
    return copies


def finish_out(me, encoded, attended, weights, count):
    frames, width = encoded.shape
    groups = len(weights)
    parts = [(3 * w, w, first) for w, first in zip(WIDTHS, STARTS)]
    tile = 256

    def body(me_ref, enc_ref, *refs):
        mixed_refs = refs[:groups]
        weight_refs = refs[groups : 2 * groups]
        out_ref, held_ref, sem = refs[2 * groups :]
        for copy in fetch(me_ref, weight_refs, held_ref, sem, parts, count):
            copy.wait()

        def one_tile(t, carry):
            part = pl.ds(pl.multiple_of(t * tile, tile), tile)
            projected = enc_ref[:, part].astype(F32)
            for mixed_ref, (_, w, first) in zip(mixed_refs, parts):
                projected = projected + dot_nt(mixed_ref[...], held_ref[part, first : first + w])
            out_ref[:, part] = projected.astype(BF16)
            return carry

        lax.fori_loop(0, width // tile, one_tile, 0)

    vmem = pl.BlockSpec(memory_space=pltpu.VMEM)
    return pl.pallas_call(
        body,
        in_specs=[
            pl.BlockSpec(memory_space=pltpu.SMEM),
            *(vmem for _ in range(1 + groups)),
            *(pl.BlockSpec(memory_space=pl.ANY) for _ in range(groups)),
        ],
        out_specs=vmem,
        out_shape=jax.ShapeDtypeStruct((frames, width), BF16),
        scratch_shapes=[
            pltpu.VMEM((width, E), BF16),
            pltpu.SemaphoreType.DMA((groups, count)),
        ],
        compiler_params=pltpu.CompilerParams(vmem_limit_bytes=24 << 20),
        cost_estimate=hint(0.1),
    )(me, encoded, *attended, *weights)


def finish_grad(me, encoded, cotangent, backs, weights, count):
    frames, width = encoded.shape
    groups = len(weights)
    parts = [(0, 3 * w, 3 * first) for w, first in zip(WIDTHS, STARTS)]
    tile = 256

    def body(me_ref, enc_ref, cot_ref, *refs):
        back_refs = refs[:groups]
        weight_refs = refs[groups : 2 * groups]
        grad_ref, held_ref, feature_ref, sem = refs[2 * groups :]
        for copy in fetch(me_ref, weight_refs, held_ref, sem, parts, count):
            copy.wait()

        def one_tile(t, carry):
            part = pl.ds(pl.multiple_of(t * tile, tile), tile)
            feature_ref[:, part] = sum(
                dot_nt(back_ref[...], held_ref[part, first : first + w])
                for back_ref, (_, w, first) in zip(back_refs, parts)
            )
            return carry

        lax.fori_loop(0, width // tile, one_tile, 0)

        def some_rows(r, carry):
            part = pl.ds(pl.multiple_of(r * 64, 64), 64)
            unit_rows, inverse = normalize_values(enc_ref[part, :].astype(F32))
            feature = feature_ref[part, :]
            centered_grad = (
                feature
                - jnp.mean(feature, axis=1, keepdims=True)
                - unit_rows * jnp.mean(feature * unit_rows, axis=1, keepdims=True)
            )
            grad_ref[part, :] = (cot_ref[part, :].astype(F32) + inverse * centered_grad).astype(BF16)
            return carry

        lax.fori_loop(0, frames // 64, some_rows, 0)

    vmem = pl.BlockSpec(memory_space=pltpu.VMEM)
    return pl.pallas_call(
        body,
        in_specs=[
            pl.BlockSpec(memory_space=pltpu.SMEM),
            *(vmem for _ in range(2 + groups)),
            *(pl.BlockSpec(memory_space=pl.ANY) for _ in range(groups)),
        ],
        out_specs=vmem,
        out_shape=jax.ShapeDtypeStruct((frames, width), BF16),
        scratch_shapes=[
            pltpu.VMEM((width, 3 * E), BF16),
            pltpu.VMEM((frames, width), F32),
            pltpu.SemaphoreType.DMA((groups, count)),
        ],
        compiler_params=pltpu.CompilerParams(vmem_limit_bytes=36 << 20),
        cost_estimate=hint(14.0),
    )(me, encoded, cotangent, *backs, *weights)


def collect(sums):
    rows = sums[0][0].shape[0]

    def body(*refs):
        outs = refs[-4:]
        at = 0
        for (_, parts), cols, first in zip(sums, WIDTHS, STARTS):
            total = refs[at][...]
            for part_ref in refs[at + 1 : at + 1 + len(parts)]:
                total = total + part_ref[...].astype(F32)
            at += 1 + len(parts)
            for k in range(4):
                outs[k][:, first : first + cols] = total[:, k * cols : (k + 1) * cols]

    flat = [a for own, parts in sums for a in (own, *parts)]
    vmem = pl.BlockSpec(memory_space=pltpu.VMEM)
    return pl.pallas_call(
        body,
        in_specs=[vmem] * len(flat),
        out_specs=[vmem] * 4,
        out_shape=[jax.ShapeDtypeStruct((rows, E), F32)] * 4,
        compiler_params=pltpu.CompilerParams(vmem_limit_bytes=16 << 20),
        cost_estimate=hint(1.2),
    )(*flat)


def shards(encoded, query_weight, key_weight, value_weight, out_weight, cotangent, valid_frames):
    valid_count = valid_frames[0]
    frames_dev = encoded.shape[0]
    count = lax.axis_size("context")
    far = count // 4
    order = order_of(count)
    index = lax.axis_index("context").astype(jnp.int32)
    first_row = index * frames_dev
    me = index[None]
    pos = jnp.stack([first_row, valid_count])
    row_mask = (first_row + jnp.arange(frames_dev, dtype=jnp.int32) < valid_count).astype(F32)[
        :, None
    ]
    left = passed_along(encoded[frames_dev - SPAN :], "context", 1)
    sources = (query_weight, key_weight, value_weight, out_weight)

    def block_of(i, sources):
        cols = WIDTHS[i]
        part = (slice(None), slice(STARTS[i], STARTS[i] + cols))
        targets = [(slice(None), slice(k * cols, (k + 1) * cols)) for k in range(4)]
        shape = (sources[0].shape[0], 4 * cols)
        return joined(sources, shape, [part] * 4, targets, 12 if i else 60)

    raw, near, other, weights = ([None] * GROUPS for _ in range(4))

    def gather_far(i, *gate):
        block = block_of(i, lax.optimization_barrier((*sources, *gate))[:4] if gate else sources)
        raw[i] = (block, *(swapped(block, 4 * k) for k in range(1, far)))

    def join_far(i, *gate):
        parts = after(raw[i], *gate) if gate else raw[i]
        near[i] = stacked(parts)

    def gather_next(i, *gate):
        if gate:
            near[i] = after(near[i], *gate)
        other[i] = swapped(near[i], 2)

    def gather_chip(i, *gate):
        if gate:
            other[i] = after(other[i], *gate)
        mine = stacked([near[i], other[i]])
        weights[i] = stacked([mine, swapped(mine, 1)])

    own_x, c, xt, ct = prepare(me, encoded, cotangent, order)
    gather_far(0)
    join_far(0, own_x)
    gather_next(0)
    near_sibling = swapped(near[0], 1)
    gather_far(1, near[0])
    join_far(1)
    other[0] = after(other[0], near[1], left)
    weights[0] = stacked([near[0], other[0], near_sibling, swapped(other[0], 1)])
    x = prepare_left(me, left, own_x, order)
    gather_next(1, other[0])
    gather_far(2, near[1], other[0])

    def project(i, *gate):
        whole = after(weights[i], *gate) if gate else weights[i]
        cols = WIDTHS[i]
        projected = jnp.dot(x, whole[:, : 3 * cols], preferred_element_type=F32).astype(BF16)
        grad_attn = jnp.dot(c, whole[:, 3 * cols :], preferred_element_type=F32)
        return projected, (grad_attn * row_mask).astype(BF16)

    attended, backs, keeps, sends, sums = [], [], [], [], []

    def sum_chip(i):
        got = swapped(sends[i], 1)
        half = got.shape[0] // 2
        held = keeps[i][:half].astype(F32) + got[:half].astype(F32)
        return held, (keeps[i][half:].astype(F32) + got[half:].astype(F32)).astype(BF16)

    def split_far(held, got):
        total = held + got.astype(F32)
        rows = total.shape[0] // far
        return total[:rows], [total[k * rows : (k + 1) * rows].astype(BF16) for k in range(1, far)]

    held = got = own = parts = None
    for i in range(GROUPS):
        projected, grad_attn = project(i, *((attended[i - 1], *other[i + 1 : i + 2]) if i else ()))
        if i:
            held, send = sum_chip(i - 1)
            held, send, projected = lax.optimization_barrier((held, send, projected))
            got = swapped(send, 2)
        if i > 1:
            parts, projected = lax.optimization_barrier((parts, projected))
            sums.append((own, parts))
        mixed, query_back, main, tail, halo = attention(pos, projected, grad_attn)
        attended.append(mixed)
        returned = passed_along(halo, "context", -1)
        if i + 1 < GROUPS:
            if i + 2 < GROUPS:
                join_far(i + 2, mixed)
            gather_chip(i + 1, mixed, *(near[i + 2 : i + 3]))
        if i + 2 < GROUPS:
            gather_next(i + 2, mixed, other[i + 1])
        if i:
            held, got, mixed = lax.optimization_barrier((held, got, mixed))
            own, away = split_far(held, got)
            parts = [swapped(part, 4 * k) for k, part in enumerate(away, 1)]
        keep, send, back = gradients(
            xt, ct, query_back, main, tail, returned, mixed, 4.0 if i + 1 < GROUPS else 0.1
        )
        keeps.append(keep)
        sends.append(send)
        backs.append(back)
    held, send = sum_chip(GROUPS - 1)
    held, send, ready = lax.optimization_barrier((held, send, me))
    got = swapped(send, 2)
    layer_out = finish_out(ready, encoded, attended, weights, count)
    got, parts, layer_out = lax.optimization_barrier((got, parts, layer_out))
    sums.append((own, parts))
    own, away = split_far(held, got)
    *away, ready = lax.optimization_barrier((*away, me))
    parts = [swapped(part, 4 * k) for k, part in enumerate(away, 1)]
    encoded_grad = finish_grad(ready, encoded, cotangent, backs, weights, count)
    parts, encoded_grad = lax.optimization_barrier((parts, encoded_grad))
    sums.append((own, parts))
    return (layer_out, encoded_grad, *collect(sums))


def solution(mesh):
    placed = (
        P(("groups", "context"), None),
        P("context", None),
        P("context", None),
        P("context", None),
        P("context", None),
        P(("groups", "context"), None),
        P("groups"),
    )
    return jax.shard_map(
        shards,
        mesh=mesh,
        in_specs=placed,
        out_specs=(P(("groups", "context"), None),) * 6,
        check_vma=False,
    )
```

```python
import jax
import jax.numpy as jnp
from jax import lax
from jax.experimental import pallas as pl
from jax.experimental.pallas import tpu as pltpu
from jax.sharding import PartitionSpec as P

HEADS = 12
HD = 64
BLOCK = 16
LEFT = 16
E = 768
SPAN = LEFT * BLOCK
HALF = SPAN // 2
PAIR = 2 * HD
SIZES = (4, 4, 4)
GROUPS = len(SIZES)
WIDTHS = tuple(HD * size for size in SIZES)
STARTS = tuple(sum(WIDTHS[:i]) for i in range(GROUPS))

epsilon = 1e-05

F32 = jnp.float32
BF16 = jnp.bfloat16

SCALE = 0.3


def hint(us):
    return pl.CostEstimate(flops=int(SCALE * us * 1.15e9), transcendentals=0, bytes_accessed=1 << 10)


def passed_along(value, axis, by):
    count = lax.axis_size(axis)
    pairs = [(i, i + by) for i in range(count) if 0 <= i + by < count]
    return lax.ppermute(value, axis, pairs)


def swapped(value, mask):
    count = lax.axis_size("context")
    return lax.ppermute(value, "context", [(i, i ^ mask) for i in range(count)])


def after(value, *others):
    return lax.optimization_barrier((value, *others))[0]


def normalize_values(values):
    centered = values - jnp.mean(values, axis=1, keepdims=True)
    inverse = lax.rsqrt(jnp.mean(centered * centered, axis=1, keepdims=True) + epsilon)
    return (centered * inverse, inverse)


def dot_nt(a, b):
    return lax.dot_general(a, b, (((1,), (1,)), ((), ())), preferred_element_type=F32)


def dot_nn(a, b):
    return lax.dot_general(a, b, (((1,), (0,)), ((), ())), preferred_element_type=F32)


def attention_body(
    pos_ref,
    q_ref,
    k_ref,
    v_ref,
    g_ref,
    o_ref,
    dq_ref,
    main_ref,
    tail_ref,
    halo_ref,
    bias_ref,
    kt_ref,
    vt_ref,
    ot_ref,
    dqt_ref,
    p_ref,
    ds_ref,
    acc_ref,
):
    rows = g_ref.shape[0]
    tiles = rows // SPAN
    first = pos_ref[0]
    count = pos_ref[1]

    @pl.when(pl.program_id(0) == 0)
    def _():
        for t in range(tiles):
            for c in range(2):
                key = lax.broadcasted_iota(jnp.int32, (SPAN + HALF, HALF), 0) + c * HALF
                query = lax.broadcasted_iota(jnp.int32, (SPAN + HALF, HALF), 1) + c * HALF
                key_block = key // BLOCK
                query_block = query // BLOCK
                pos = key + (first + (t - 1) * SPAN)
                allowed = (
                    (key_block >= query_block)
                    & (key_block <= query_block + LEFT)
                    & (pos >= 0)
                    & (pos < count)
                )
                bias_ref[t, c] = jnp.where(allowed, 0.0, -1e30)
        p_ref[...] = jnp.zeros_like(p_ref)
        ds_ref[...] = jnp.zeros_like(ds_ref)

    kt_ref[...] = k_ref[...].T
    vt_ref[...] = v_ref[...].T
    lane = lax.broadcasted_iota(jnp.int32, (SPAN, PAIR), 1)
    acc_ref[...] = jnp.zeros_like(acc_ref)

    def one_tile(t, carry):
        start = pl.multiple_of(t * SPAN, SPAN)
        qs = pl.ds(start, SPAN)
        ks = pl.ds(start, 2 * SPAN)
        q = q_ref[pl.ds(start + SPAN, SPAN), :] * BF16(HD ** (-0.5))
        g = g_ref[qs, :]
        k = k_ref[ks, :]
        v = v_ref[ks, :]
        q_heads = []
        g_heads = []
        for h in range(2):
            mine = (lane >= HD) if h else (lane < HD)
            q_heads.append(jnp.where(mine, q, jnp.zeros_like(q)))
            g_heads.append(jnp.where(mine, g, jnp.zeros_like(g)))
            s = dot_nt(k, q_heads[h])
            d = dot_nt(v, g_heads[h])
            for c in range(2):
                kr = slice(c * HALF, c * HALF + SPAN + HALF)
                qc = slice(c * HALF, (c + 1) * HALF)
                out = slice(h * SPAN + c * HALF, h * SPAN + (c + 1) * HALF)
                scores = s[kr, qc] + bias_ref[t, c]
                shifted = jnp.exp(scores - jnp.max(scores, axis=0, keepdims=True))
                probs = shifted * (1.0 / jnp.sum(shifted, axis=0, keepdims=True))
                weighted = probs * d[kr, qc]
                delta = jnp.sum(weighted, axis=0, keepdims=True)
                p_ref[kr, out] = probs.astype(BF16)
                ds_ref[kr, out] = (weighted - probs * delta).astype(BF16)
            hs = slice(h * HD, (h + 1) * HD)
            cols = slice(h * SPAN, (h + 1) * SPAN)
            ot_ref[hs, qs] = dot_nn(vt_ref[hs, ks], p_ref[:, cols])
            dqt_ref[hs, qs] = dot_nn(kt_ref[hs, ks], ds_ref[:, cols]) * HD ** (-0.5)
        acc_ref[0, ks, :] += dot_nn(ds_ref[...], jnp.concatenate(q_heads, axis=0))
        acc_ref[1, ks, :] += dot_nn(p_ref[...], jnp.concatenate(g_heads, axis=0))
        return carry

    lax.fori_loop(0, tiles, one_tile, 0, unroll=True)
    row = lax.broadcasted_iota(jnp.int32, (rows, PAIR), 0) + first
    o_ref[...] = jnp.where(row < count, ot_ref[...].T, 0.0).astype(BF16)
    dq_ref[...] = dqt_ref[...].T.astype(BF16)
    halo_ref[...] = acc_ref[:, :SPAN, :].astype(BF16)
    main_ref[...] = acc_ref[:, SPAN:rows, :].astype(BF16)
    tail_ref[...] = acc_ref[:, rows:, :]


def attention(pos, projected, grad_attn):
    rows, cols = grad_attn.shape
    ext = rows + SPAN
    steps = cols // PAIR
    sd = jax.ShapeDtypeStruct
    column = lambda part: pl.BlockSpec((ext, PAIR), lambda j: (0, part * steps + j))
    flat = pl.BlockSpec((rows, PAIR), lambda j: (0, j))
    both = lambda r: pl.BlockSpec((2, r, PAIR), lambda j: (0, 0, j))
    return pl.pallas_call(
        attention_body,
        grid=(steps,),
        in_specs=[pl.BlockSpec(memory_space=pltpu.SMEM), column(0), column(1), column(2), flat],
        out_specs=[flat, flat, both(rows - SPAN), both(SPAN), both(SPAN)],
        out_shape=[
            sd((rows, cols), BF16),
            sd((rows, cols), BF16),
            sd((2, rows - SPAN, cols), BF16),
            sd((2, SPAN, cols), F32),
            sd((2, SPAN, cols), BF16),
        ],
        scratch_shapes=[
            pltpu.VMEM((rows // SPAN, 2, SPAN + HALF, HALF), F32),
            pltpu.VMEM((PAIR, ext), BF16),
            pltpu.VMEM((PAIR, ext), BF16),
            pltpu.VMEM((PAIR, rows), F32),
            pltpu.VMEM((PAIR, rows), F32),
            pltpu.VMEM((2 * SPAN, 2 * SPAN), BF16),
            pltpu.VMEM((2 * SPAN, 2 * SPAN), BF16),
            pltpu.VMEM((2, ext, PAIR), F32),
        ],
        compiler_params=pltpu.CompilerParams(
            dimension_semantics=("arbitrary",), vmem_limit_bytes=24 << 20
        ),
        cost_estimate=hint(9.4),
    )(pos, projected, projected, projected, grad_attn)


def order_of(count):
    if count < 4 or count & (count - 1):
        raise ValueError("context size")
    far = count // 4
    return [4 * k + 2 * y + c for c in range(2) for y in range(2) for k in range(far)]


def joined(parts, shape, sources, targets, grant=12):
    def body(*refs):
        out_ref, sem = refs[-2:]
        copies = [
            pltpu.make_async_copy(ref.at[source], out_ref.at[target], sem.at[i])
            for i, (ref, source, target) in enumerate(zip(refs[:-2], sources, targets))
        ]
        for copy in copies:
            copy.start()
        for copy in copies:
            copy.wait()

    return pl.pallas_call(
        body,
        in_specs=[pl.BlockSpec(memory_space=pltpu.HBM)] * len(parts),
        out_specs=pl.BlockSpec(memory_space=pltpu.VMEM),
        out_shape=jax.ShapeDtypeStruct(shape, parts[0].dtype),
        scratch_shapes=[pltpu.SemaphoreType.DMA((len(parts),))],
        compiler_params=pltpu.CompilerParams(vmem_limit_bytes=grant << 20),
        cost_estimate=hint(1.5),
    )(*parts)


def stacked(parts):
    ends = [sum(p.shape[0] for p in parts[: i + 1]) for i in range(len(parts))]
    whole = [(slice(None), slice(None))] * len(parts)
    targets = [(slice(end - p.shape[0], end), slice(None)) for end, p in zip(ends, parts)]
    return joined(parts, (ends[-1], parts[0].shape[1]), whole, targets)


def put_in_order(out_ref, flat_ref, turned_ref, value, here, order):
    rows = turned_ref.shape[0] // len(order)
    turned_ref[...] = value.T
    for j, offset in enumerate(order):
        source = pl.multiple_of((here ^ offset) * rows, rows)
        out_ref[j * rows : (j + 1) * rows, :] = turned_ref[pl.ds(source, rows), :]
    flat_ref[...] = out_ref[...].T


def prepare(me, encoded, cotangent, order):
    frames, width = encoded.shape

    def body(me_ref, own_ref, cot_ref, x_ref, c_ref, xt_ref, ct_ref, turned_ref):
        here = me_ref[0]
        normed = normalize_values(own_ref[...].astype(F32))[0].astype(BF16)
        put_in_order(xt_ref, x_ref, turned_ref, normed, here, order)
        put_in_order(ct_ref, c_ref, turned_ref, cot_ref[...], here, order)

    sd = jax.ShapeDtypeStruct
    flat = pl.BlockSpec((SPAN, width), lambda i: (i, 0))
    turned = pl.BlockSpec((width, SPAN), lambda i: (0, i))
    return pl.pallas_call(
        body,
        grid=(frames // SPAN,),
        in_specs=[pl.BlockSpec(memory_space=pltpu.SMEM), flat, flat],
        out_specs=[pl.BlockSpec((SPAN, width), lambda i: (i + 1, 0)), flat, turned, turned],
        out_shape=[
            sd((frames + SPAN, width), BF16),
            sd((frames, width), BF16),
            sd((width, frames), BF16),
            sd((width, frames), BF16),
        ],
        scratch_shapes=[pltpu.VMEM((width, SPAN), BF16)],
        compiler_params=pltpu.CompilerParams(
            dimension_semantics=("arbitrary",), vmem_limit_bytes=60 << 20
        ),
        cost_estimate=hint(6.4),
    )(me, encoded, cotangent)


def prepare_left(me, left, x, order):
    width = left.shape[1]

    def body(me_ref, left_ref, x_ref, out_ref, ordered_ref, turned_ref):
        normed = normalize_values(left_ref[...].astype(F32))[0].astype(BF16)
        put_in_order(ordered_ref, out_ref, turned_ref, normed, me_ref[0], order)

    return pl.pallas_call(
        body,
        grid=(1,),
        in_specs=[
            pl.BlockSpec(memory_space=pltpu.SMEM),
            pl.BlockSpec((SPAN, width), lambda i: (0, 0)),
            pl.BlockSpec(memory_space=pl.ANY),
        ],
        out_specs=pl.BlockSpec((SPAN, width), lambda i: (0, 0)),
        out_shape=jax.ShapeDtypeStruct(x.shape, x.dtype),
        input_output_aliases={2: 0},
        scratch_shapes=[pltpu.VMEM((width, SPAN), BF16), pltpu.VMEM((width, SPAN), BF16)],
        compiler_params=pltpu.CompilerParams(vmem_limit_bytes=12 << 20),
        cost_estimate=hint(2.0),
    )(me, left, x)


def gradients_body(
    xt_ref, ct_ref, query_ref, main_ref, tail_ref, returned_ref, mixed_ref, keep_ref, send_ref, back_ref
):
    step = pl.program_id(0)
    half = pl.num_programs(0) // 2
    rows, cols = query_ref.shape

    @pl.when(step == 0)
    def _():
        back_ref[:, :cols] = query_ref[...]
        for i in range(2):
            part = slice((i + 1) * cols, (i + 2) * cols)
            back_ref[: rows - SPAN, part] = main_ref[i]
            back_ref[rows - SPAN :, part] = (tail_ref[i] + returned_ref[i].astype(F32)).astype(BF16)

    inner = dot_nn(xt_ref[...], back_ref[...]).astype(BF16)
    outer = dot_nn(ct_ref[...], mixed_ref[...]).astype(BF16)

    @pl.when(step < half)
    def _():
        keep_ref[:, : 3 * cols] = inner
        keep_ref[:, 3 * cols :] = outer

    @pl.when(step >= half)
    def _():
        send_ref[:, : 3 * cols] = inner
        send_ref[:, 3 * cols :] = outer


def gradients(xt, ct, query_back, main, tail, returned, mixed, us):
    width = xt.shape[0]
    rows, cols = mixed.shape
    tile = 384
    steps = width // tile
    whole = lambda a: pl.BlockSpec(a.shape, lambda i: (0,) * a.ndim)
    sd = jax.ShapeDtypeStruct
    return pl.pallas_call(
        gradients_body,
        grid=(steps,),
        in_specs=[
            pl.BlockSpec((tile, rows), lambda i: (i, 0)),
            pl.BlockSpec((tile, rows), lambda i: (i, 0)),
            *(whole(a) for a in (query_back, main, tail, returned, mixed)),
        ],
        out_specs=[
            pl.BlockSpec((tile, 4 * cols), lambda i: (jnp.minimum(i, steps // 2 - 1), 0)),
            pl.BlockSpec((tile, 4 * cols), lambda i: (jnp.maximum(i - steps // 2, 0), 0)),
            pl.BlockSpec((rows, 3 * cols), lambda i: (0, 0)),
        ],
        out_shape=[
            sd((width // 2, 4 * cols), BF16),
            sd((width // 2, 4 * cols), BF16),
            sd((rows, 3 * cols), BF16),
        ],
        compiler_params=pltpu.CompilerParams(
            dimension_semantics=("arbitrary",), vmem_limit_bytes=24 << 20
        ),
        cost_estimate=hint(us),
    )(xt, ct, query_back, main, tail, returned, mixed)


def fetch(me_ref, weight_refs, held_ref, sem, parts, count):
    here = me_ref[0]
    rows = held_ref.shape[0] // count
    copies = []
    for d in range(count):
        apart = here ^ d
        j = apart % 2 * (count // 2) + apart // 2 % 2 * (count // 4) + apart // 4
        source = pl.multiple_of(j * rows, rows)
        for g, (weight_ref, (first, cols, to)) in enumerate(zip(weight_refs, parts)):
            copies.append(
                pltpu.make_async_copy(
                    weight_ref.at[pl.ds(source, rows), first : first + cols],
                    held_ref.at[d * rows : (d + 1) * rows, to : to + cols],
                    sem.at[g, d],
                )
            )
    for copy in copies:
        copy.start()
    return copies


def finish_out(me, encoded, attended, weights, count):
    frames, width = encoded.shape
    groups = len(weights)
    parts = [(3 * w, w, first) for w, first in zip(WIDTHS, STARTS)]
    tile = 256

    def body(me_ref, enc_ref, *refs):
        mixed_refs = refs[:groups]
        weight_refs = refs[groups : 2 * groups]
        out_ref, held_ref, sem = refs[2 * groups :]
        for copy in fetch(me_ref, weight_refs, held_ref, sem, parts, count):
            copy.wait()

        def one_tile(t, carry):
            part = pl.ds(pl.multiple_of(t * tile, tile), tile)
            projected = enc_ref[:, part].astype(F32)
            for mixed_ref, (_, w, first) in zip(mixed_refs, parts):
                projected = projected + dot_nt(mixed_ref[...], held_ref[part, first : first + w])
            out_ref[:, part] = projected.astype(BF16)
            return carry

        lax.fori_loop(0, width // tile, one_tile, 0)

    vmem = pl.BlockSpec(memory_space=pltpu.VMEM)
    return pl.pallas_call(
        body,
        in_specs=[
            pl.BlockSpec(memory_space=pltpu.SMEM),
            *(vmem for _ in range(1 + groups)),
            *(pl.BlockSpec(memory_space=pl.ANY) for _ in range(groups)),
        ],
        out_specs=vmem,
        out_shape=jax.ShapeDtypeStruct((frames, width), BF16),
        scratch_shapes=[
            pltpu.VMEM((width, E), BF16),
            pltpu.SemaphoreType.DMA((groups, count)),
        ],
        compiler_params=pltpu.CompilerParams(vmem_limit_bytes=24 << 20),
        cost_estimate=hint(0.1),
    )(me, encoded, *attended, *weights)


def finish_grad(me, encoded, cotangent, backs, weights, count):
    frames, width = encoded.shape
    groups = len(weights)
    parts = [(0, 3 * w, 3 * first) for w, first in zip(WIDTHS, STARTS)]
    tile = 256

    def body(me_ref, enc_ref, cot_ref, *refs):
        back_refs = refs[:groups]
        weight_refs = refs[groups : 2 * groups]
        grad_ref, held_ref, feature_ref, sem = refs[2 * groups :]
        for copy in fetch(me_ref, weight_refs, held_ref, sem, parts, count):
            copy.wait()

        def one_tile(t, carry):
            part = pl.ds(pl.multiple_of(t * tile, tile), tile)
            feature_ref[:, part] = sum(
                dot_nt(back_ref[...], held_ref[part, first : first + w])
                for back_ref, (_, w, first) in zip(back_refs, parts)
            )
            return carry

        lax.fori_loop(0, width // tile, one_tile, 0)

        def some_rows(r, carry):
            part = pl.ds(pl.multiple_of(r * 64, 64), 64)
            unit_rows, inverse = normalize_values(enc_ref[part, :].astype(F32))
            feature = feature_ref[part, :]
            centered_grad = (
                feature
                - jnp.mean(feature, axis=1, keepdims=True)
                - unit_rows * jnp.mean(feature * unit_rows, axis=1, keepdims=True)
            )
            grad_ref[part, :] = (cot_ref[part, :].astype(F32) + inverse * centered_grad).astype(BF16)
            return carry

        lax.fori_loop(0, frames // 64, some_rows, 0)

    vmem = pl.BlockSpec(memory_space=pltpu.VMEM)
    return pl.pallas_call(
        body,
        in_specs=[
            pl.BlockSpec(memory_space=pltpu.SMEM),
            *(vmem for _ in range(2 + groups)),
            *(pl.BlockSpec(memory_space=pl.ANY) for _ in range(groups)),
        ],
        out_specs=vmem,
        out_shape=jax.ShapeDtypeStruct((frames, width), BF16),
        scratch_shapes=[
            pltpu.VMEM((width, 3 * E), BF16),
            pltpu.VMEM((frames, width), F32),
            pltpu.SemaphoreType.DMA((groups, count)),
        ],
        compiler_params=pltpu.CompilerParams(vmem_limit_bytes=36 << 20),
        cost_estimate=hint(14.0),
    )(me, encoded, cotangent, *backs, *weights)


def collect(sums):
    rows = sums[0][0].shape[0]

    def body(*refs):
        outs = refs[-4:]
        at = 0
        for (_, parts), cols, first in zip(sums, WIDTHS, STARTS):
            total = refs[at][...]
            for part_ref in refs[at + 1 : at + 1 + len(parts)]:
                total = total + part_ref[...].astype(F32)
            at += 1 + len(parts)
            for k in range(4):
                outs[k][:, first : first + cols] = total[:, k * cols : (k + 1) * cols]

    flat = [a for own, parts in sums for a in (own, *parts)]
    vmem = pl.BlockSpec(memory_space=pltpu.VMEM)
    return pl.pallas_call(
        body,
        in_specs=[vmem] * len(flat),
        out_specs=[vmem] * 4,
        out_shape=[jax.ShapeDtypeStruct((rows, E), F32)] * 4,
        compiler_params=pltpu.CompilerParams(vmem_limit_bytes=16 << 20),
        cost_estimate=hint(1.2),
    )(*flat)


def shards(encoded, query_weight, key_weight, value_weight, out_weight, cotangent, valid_frames):
    valid_count = valid_frames[0]
    frames_dev = encoded.shape[0]
    count = lax.axis_size("context")
    far = count // 4
    order = order_of(count)
    index = lax.axis_index("context").astype(jnp.int32)
    first_row = index * frames_dev
    me = index[None]
    pos = jnp.stack([first_row, valid_count])
    row_mask = (first_row + jnp.arange(frames_dev, dtype=jnp.int32) < valid_count).astype(F32)[
        :, None
    ]
    left = passed_along(encoded[frames_dev - SPAN :], "context", 1)
    sources = (query_weight, key_weight, value_weight, out_weight)

    def block_of(i, sources):
        cols = WIDTHS[i]
        part = (slice(None), slice(STARTS[i], STARTS[i] + cols))
        targets = [(slice(None), slice(k * cols, (k + 1) * cols)) for k in range(4)]
        shape = (sources[0].shape[0], 4 * cols)
        return joined(sources, shape, [part] * 4, targets, 12 if i else 60)

    raw, near, other, weights = ([None] * GROUPS for _ in range(4))

    def gather_far(i, *gate):
        block = block_of(i, lax.optimization_barrier((*sources, *gate))[:4] if gate else sources)
        raw[i] = (block, *(swapped(block, 4 * k) for k in range(1, far)))

    def join_far(i, *gate):
        parts = after(raw[i], *gate) if gate else raw[i]
        near[i] = stacked(parts)

    def gather_next(i, *gate):
        if gate:
            near[i] = after(near[i], *gate)
        other[i] = swapped(near[i], 2)

    def gather_chip(i, *gate):
        if gate:
            other[i] = after(other[i], *gate)
        mine = stacked([near[i], other[i]])
        weights[i] = stacked([mine, swapped(mine, 1)])

    own_x, c, xt, ct = prepare(me, encoded, cotangent, order)
    gather_far(0)
    join_far(0, own_x)
    gather_next(0)
    near_sibling = swapped(near[0], 1)
    gather_far(1, near[0])
    join_far(1)
    other[0] = after(other[0], near[1], left)
    weights[0] = stacked([near[0], other[0], near_sibling, swapped(other[0], 1)])
    x = prepare_left(me, left, own_x, order)
    gather_next(1, other[0])
    gather_far(2, near[1], other[0])

    def project(i, *gate):
        whole = after(weights[i], *gate) if gate else weights[i]
        cols = WIDTHS[i]
        projected = jnp.dot(x, whole[:, : 3 * cols], preferred_element_type=F32).astype(BF16)
        grad_attn = jnp.dot(c, whole[:, 3 * cols :], preferred_element_type=F32)
        return projected, (grad_attn * row_mask).astype(BF16)

    attended, backs, keeps, sends, sums = [], [], [], [], []

    def sum_chip(i):
        got = swapped(sends[i], 1)
        half = got.shape[0] // 2
        held = keeps[i][:half].astype(F32) + got[:half].astype(F32)
        return held, (keeps[i][half:].astype(F32) + got[half:].astype(F32)).astype(BF16)

    def split_far(held, got):
        total = held + got.astype(F32)
        rows = total.shape[0] // far
        return total[:rows], [total[k * rows : (k + 1) * rows].astype(BF16) for k in range(1, far)]

    held = got = own = parts = None
    for i in range(GROUPS):
        projected, grad_attn = project(i, *((attended[i - 1], *other[i + 1 : i + 2]) if i else ()))
        if i:
            held, send = sum_chip(i - 1)
            held, send, projected = lax.optimization_barrier((held, send, projected))
            got = swapped(send, 2)
        if i > 1:
            parts, projected = lax.optimization_barrier((parts, projected))
            sums.append((own, parts))
        mixed, query_back, main, tail, halo = attention(pos, projected, grad_attn)
        attended.append(mixed)
        returned = passed_along(halo, "context", -1)
        if i + 1 < GROUPS:
            if i + 2 < GROUPS:
                join_far(i + 2, mixed)
            gather_chip(i + 1, mixed, *(near[i + 2 : i + 3]))
        if i + 2 < GROUPS:
            gather_next(i + 2, mixed, other[i + 1])
        if i:
            held, got, mixed = lax.optimization_barrier((held, got, mixed))
            own, away = split_far(held, got)
            parts = [swapped(part, 4 * k) for k, part in enumerate(away, 1)]
        keep, send, back = gradients(
            xt, ct, query_back, main, tail, returned, mixed, 4.0 if i + 1 < GROUPS else 0.1
        )
        keeps.append(keep)
        sends.append(send)
        backs.append(back)
    held, send = sum_chip(GROUPS - 1)
    held, send, ready = lax.optimization_barrier((held, send, me))
    got = swapped(send, 2)
    layer_out = finish_out(ready, encoded, attended, weights, count)
    got, parts, layer_out = lax.optimization_barrier((got, parts, layer_out))
    sums.append((own, parts))
    own, away = split_far(held, got)
    *away, ready = lax.optimization_barrier((*away, me))
    parts = [swapped(part, 4 * k) for k, part in enumerate(away, 1)]
    encoded_grad = finish_grad(ready, encoded, cotangent, backs, weights, count)
    parts, encoded_grad = lax.optimization_barrier((parts, encoded_grad))
    sums.append((own, parts))
    return (layer_out, encoded_grad, *collect(sums))


def solution(mesh):
    placed = (
        P(("groups", "context"), None),
        P("context", None),
        P("context", None),
        P("context", None),
        P("context", None),
        P(("groups", "context"), None),
        P("groups"),
    )
    return jax.shard_map(
        shards,
        mesh=mesh,
        in_specs=placed,
        out_specs=(P(("groups", "context"), None),) * 6,
        check_vma=False,
    )
```
